128 devices in a mesh: tm: 16 (over z, y), height: 8 (over x, core).
Axes of the slice: x: 4, y: 4, z: 4, core: 2. Of those that a mesh axis runs over, the one named last changes fastest.
Arguments:
- latents: bfloat16 [32, 32, 128, 256], P('tm', 'height'), may hold values from -6 to 6
- conv_first: bfloat16 [3, 3, 3, 256, 256], replicated, may hold values from -0.078125 to 0.078125
- conv_second: bfloat16 [3, 3, 3, 256, 256], replicated, may hold values from -0.078125 to 0.078125
- codebook: bfloat16 [262144, 256], P('height'), may hold values from -13 to 13
- codes: int32 [32, 32, 128], P('tm', 'height'), may hold values from 0 to 262143, as said below
- upstream: bfloat16 [32, 32, 128, 256], P('tm', 'height'), may hold values from -6 to 6
Outputs:
- grad_latent: bfloat16 [32, 32, 128, 256], P('tm', 'height')
- codebook_grad: bfloat16 [262144, 256], P(('height', 'tm'))
The draws below stay inside these ranges and needn't reach their ends.
Inputs may be any that keep to these rules, and one draw needn't show every extreme that they name: Each device's 1024 cells hold at most 16 codes of any one aligned range of 2048 codes; some ranges receive exactly 16 from every device.
All inputs are finite; a program needn't handle non-finite values.
Results may differ from the reference program's by a relative error of at most 0.0085.
Values may be sent and summed in bfloat16 or wider, within the bound.
A program may use at most 128 MiB of HBM per device.

```python
import jax
import jax.numpy as jnp
from jax import lax

C = 256
K = 262144
T_DEV = 2
H_DEV = 4
W = 128
TT = 32
HH = 32
CELLS_DEV = 1024
CAP = 16
K_OWN = 2048
N_TM = 16
N_HEIGHT = 8


def draw_codebook(key, part):
    key_base, key_col, key_row = jax.random.split(key, 3)
    column_scale = jnp.exp(jax.random.uniform(key_col, (1, C), jnp.float32, -1.15, 1.15))
    row_scale = jnp.exp(jax.random.uniform(key_row, (K, 1), jnp.float32, -0.7, 0.7))
    base = jnp.clip(jax.random.normal(key_base, (K, C), jnp.float32), -4.0, 4.0)
    values = base * row_scale * column_scale * 0.5
    return values.astype(jnp.bfloat16)


def draw_codes(key, part):
    owners = N_TM * N_HEIGHT
    slots = owners * CAP
    key_rank, key_noise, key_order, key_first, key_second = jax.random.split(key, 5)
    ranking = jax.random.permutation(key_rank, owners).astype(jnp.int32)
    priority = jnp.where(ranking < owners // 8, 4096, ranking * 256 // owners).astype(jnp.int32)
    slot_owner = (jnp.arange(slots, dtype=jnp.int32) // CAP).astype(jnp.int32)
    noise = jax.random.randint(key_noise, (owners, slots), 0, 1024, dtype=jnp.int32)
    score = (priority[slot_owner][None, :] + noise) * slots + jnp.arange(slots, dtype=jnp.int32)[None, :]
    picked = lax.top_k(score, CELLS_DEV)[1].astype(jnp.int32)
    chosen = slot_owner[picked]
    order_keys = jax.random.split(key_order, owners)
    order = jax.vmap(lambda order_key: jax.random.permutation(order_key, CELLS_DEV).astype(jnp.int32))(order_keys)
    chosen = jnp.take_along_axis(chosen, order, 1)
    offset = jnp.minimum(jax.random.randint(key_first, (owners, CELLS_DEV), 0, K_OWN, dtype=jnp.int32), jax.random.randint(key_second, (owners, CELLS_DEV), 0, K_OWN, dtype=jnp.int32))
    values = chosen * K_OWN + offset
    values = values.reshape(N_TM, N_HEIGHT, T_DEV, H_DEV, W).transpose(0, 2, 1, 3, 4)
    return values.reshape(TT, HH, W).astype(jnp.int32)


def block_levels(key, extent, cuts, low, largest):
    def one(axis_at, parts):
        steps = jax.random.uniform(jax.random.fold_in(jax.random.fold_in(key, 6), axis_at), (parts,), jnp.float32, low / len(cuts), largest / len(cuts))
        return jnp.repeat(jnp.exp(steps), extent[axis_at] // parts).reshape((-1,) + (1,) * (len(extent) - axis_at - 1))

    factor_of = one(*cuts[0])
    for cut in cuts[1:]:
        factor_of = factor_of * one(*cut)
    return factor_of


def gaussian(own_key, dims, scale, bound, cuts=(), kind=jnp.bfloat16):
    level = block_levels(own_key, dims, cuts, -0.22, 0.18) if cuts else 1.0
    array = jax.random.normal(own_key, dims, jnp.float32) * scale * level
    return jnp.minimum(jnp.maximum(array, -bound), bound).astype(kind)


def setup_inputs(seed: int = 0) -> dict:
    arg_keys = jax.random.split(jax.random.key(seed), 7)
    latents = gaussian(arg_keys[0], (TT, HH, W, C), 1.0, 6.0, ((0, 16), (1, 8)))
    conv_first = gaussian(arg_keys[1], (3, 3, 3, C, C), (27 * C) ** -0.5, 0.078125)
    conv_second = gaussian(arg_keys[2], (3, 3, 3, C, C), (27 * C) ** -0.5, 0.078125)
    codebook = draw_codebook(jax.random.fold_in(arg_keys[6], 71), 0)
    codes = draw_codes(jax.random.fold_in(arg_keys[6], 71), 0)
    upstream = gaussian(arg_keys[5], (TT, HH, W, C), 1.0, 6.0, ((0, 16), (1, 8)))
    return {"latents": latents, "conv_first": conv_first, "conv_second": conv_second, "codebook": codebook, "codes": codes, "upstream": upstream}


COMMIT = 0.25

def norm_act(video):
    values = video.astype(jnp.float32)
    scaled = values * lax.rsqrt(lax.optimization_barrier(jnp.mean(values * values, -1, keepdims=True)) + 1e-06)
    return jax.nn.silu(scaled).astype(jnp.bfloat16)

def conv_block(video, weight):
    active = norm_act(video)
    padded = jnp.pad(active, ((2, 0), (1, 1), (1, 1), (0, 0)))
    flat_weight = weight.reshape(27 * C, C)

    def one_frame(frame):
        window = lax.dynamic_slice_in_dim(padded, frame.astype(jnp.int32), 3, 0)
        pieces = [window[step_t, step_h:step_h + HH, step_w:step_w + W, :] for step_t in range(3) for step_h in range(3) for step_w in range(3)]
        patch = jnp.concatenate(pieces, -1).reshape(HH * W, 27 * C)
        return jnp.dot(patch, flat_weight, preferred_element_type=jnp.float32).reshape(HH, W, C)
    conv = lax.map(one_frame, jnp.arange(TT, dtype=jnp.int32))
    return (video.astype(jnp.float32) + conv).astype(jnp.bfloat16)

def rotate_back(latent, quant, upward):
    lat_norm = jnp.sqrt(lax.optimization_barrier(jnp.sum(latent * latent, -1, keepdims=True)) + 1e-06)
    quant_norm = jnp.sqrt(lax.optimization_barrier(jnp.sum(quant * quant, -1, keepdims=True)) + 1e-06)
    lat_unit = latent / lat_norm
    quant_unit = quant / quant_norm
    cosine = lax.optimization_barrier(jnp.sum(lat_unit * quant_unit, -1, keepdims=True))
    summed = lat_unit + quant_unit
    turned = upward - summed * (lax.optimization_barrier(jnp.sum(summed * upward, -1, keepdims=True)) / (1.0 + cosine))
    turned = turned + 2.0 * lat_unit * lax.optimization_barrier(jnp.sum(quant_unit * upward, -1, keepdims=True))
    return quant_norm / lat_norm * turned + 2.0 * COMMIT * (latent - quant)

def reference(latents, conv_first, conv_second, codebook, codes, upstream):
    first = conv_block(latents, conv_first)
    encoded = conv_block(first, conv_second)
    code_flat = codes.reshape(-1).astype(jnp.int32)
    latent_flat = encoded.reshape(-1, C).astype(jnp.float32)
    quant = jnp.take(codebook, code_flat, axis=0).astype(jnp.float32)
    upward = upstream.reshape(-1, C).astype(jnp.float32)
    grad_flat = rotate_back(latent_flat, quant, upward)
    diff = lax.optimization_barrier((quant - latent_flat).astype(jnp.bfloat16))
    sums = jax.ops.segment_sum(diff.astype(jnp.float32), code_flat, num_segments=K)
    grad_latent = grad_flat.astype(jnp.bfloat16).reshape(upstream.shape)
    return (grad_latent, (2.0 * sums).astype(jnp.bfloat16))
```

```python
import functools

import jax
import jax.numpy as jnp
from jax import lax
from jax.experimental import pallas as pl
from jax.experimental.pallas import tpu as pltpu
from jax.sharding import PartitionSpec as P

F32 = jnp.float32
BF16 = jnp.bfloat16
I32 = jnp.int32
MESH = pl.DeviceIdType.MESH
C = 256
NT, NH = 16, 8
OWN = NT * NH
CAP = 16
SLOTS = OWN * CAP
K_OWN = 2048
CELLS = 1024
VMEM_LIMIT = 60 * 1024 * 1024


def onehot(cond):
    return jnp.where(cond, 1.0, 0.0).astype(BF16)


def slots_kernel(codes_ref, msg_ref, slot_ref):
    codes = codes_ref[...]
    blk = lax.shift_right_logical(codes, 11)
    off1 = jnp.bitwise_and(codes, K_OWN - 1) + 1
    sub = lax.broadcasted_iota(I32, (OWN, 128), 0)
    ht = jnp.concatenate(
        [onehot(sub == jnp.broadcast_to(blk[j : j + 1, :], (OWN, 128))) for j in range(8)], 1
    )
    upper = onehot(
        lax.broadcasted_iota(I32, (CELLS, CELLS), 0) < lax.broadcasted_iota(I32, (CELLS, CELLS), 1)
    )
    before = jnp.dot(ht, upper, preferred_element_type=F32)
    rank_row = jnp.sum(before * ht.astype(F32), axis=0, keepdims=True)
    rank = jnp.concatenate([rank_row[:, j * 128 : (j + 1) * 128] for j in range(8)], 0)
    slot_ref[...] = blk * CAP + rank.astype(I32)
    hi = lax.shift_right_logical(off1, 6).astype(F32)
    lo = jnp.bitwise_and(off1, 63).astype(F32)
    lane16 = jnp.bitwise_and(lax.broadcasted_iota(I32, (128, 128), 1), CAP - 1).astype(F32)
    v_hi, v_lo = [], []
    for j in range(8):

        def column(x):
            return jnp.transpose(jnp.broadcast_to(x[j : j + 1, :], (128, 128)))

        match = column(rank) == lane16
        v_hi.append(jnp.where(match, column(hi), 0.0).astype(BF16))
        v_lo.append(jnp.where(match, column(lo), 0.0).astype(BF16))
    m_hi = jnp.dot(ht, jnp.concatenate(v_hi, 0), preferred_element_type=F32)
    m_lo = jnp.dot(ht, jnp.concatenate(v_lo, 0), preferred_element_type=F32)
    msg_ref[...] = (m_hi * 64.0 + m_lo).astype(I32)


def make_slots(codes):
    vm = pl.BlockSpec(memory_space=pltpu.VMEM)
    return pl.pallas_call(
        slots_kernel,
        out_shape=(
            jax.ShapeDtypeStruct((OWN, 128), I32),
            jax.ShapeDtypeStruct((8, 128), I32),
        ),
        in_specs=[vm],
        out_specs=(vm, vm),
        compiler_params=pltpu.CompilerParams(vmem_limit_bytes=VMEM_LIMIT),
        name="slots",
    )(codes)


def norm_act(values):
    scaled = values * lax.rsqrt(jnp.mean(values * values, -1, keepdims=True) + 1e-06)
    return (scaled / (1.0 + jnp.exp(-scaled))).astype(BF16)


def conv_kernel(
    lat_ref,
    w1_ref,
    w2_ref,
    msg_ref,
    book_ref,
    enc_ref,
    rows_ref,
    wv,
    ext,
    cat,
    acc,
    first,
    rcodes,
    cbuf,
    sbuf,
    rbuf,
    w_sem,
    xs_sem,
    xr_sem,
    ts_sem,
    tr_sem,
    cs_sem,
    cr_sem,
    cb_sem,
    rs_sem,
    rr_sem,
    out_sem,
):
    t = lax.axis_index("tm")
    h = lax.axis_index("height")
    t_next, t_prev = lax.rem(t + 1, NT), lax.rem(t + NT - 1, NT)
    h_up, h_down = lax.rem(h + NH - 1, NH), lax.rem(h + 1, NH)

    barrier = pltpu.get_barrier_semaphore()
    pl.semaphore_signal(barrier, inc=1, device_id=(t_next, h), device_id_type=MESH)
    pl.semaphore_signal(barrier, inc=1, device_id=(t_prev, h), device_id_type=MESH)
    for i in range(1, NH):
        pl.semaphore_signal(
            barrier, inc=1, device_id=(t, lax.rem(h + i, NH)), device_id_type=MESH
        )

    for c, w_ref in enumerate((w1_ref, w2_ref)):
        for p in (2, 1, 0):
            for q in range(3):
                for r in range(3):
                    pltpu.make_async_copy(
                        w_ref.at[p, q, r],
                        wv.at[c, p, pl.ds(q * C, C), pl.ds(r * C, C)],
                        w_sem.at[c, p],
                    ).start()

    def weights_here(c, p):
        pltpu.make_async_copy(wv.at[c, p], wv.at[c, p], w_sem.at[c, p]).wait()

    def book_copy(g):
        return pltpu.make_async_copy(
            book_ref.at[pl.ds(g * K_OWN, K_OWN)], cbuf.at[g % 4], cb_sem.at[g % 4]
        )

    for g in range(4):
        book_copy(g).start()

    def x_copy(c, e, d):
        src, dst, to = ((1, 5, h_up), (4, 0, h_down))[d]
        return pltpu.make_async_remote_copy(
            src_ref=ext.at[c, e, src],
            dst_ref=ext.at[c, e, dst],
            send_sem=xs_sem.at[c, e, d],
            recv_sem=xr_sem.at[c, e, d],
            device_id=(t, to),
            device_id_type=MESH,
        )

    def t_copy(c, e):
        return pltpu.make_async_remote_copy(
            src_ref=ext.at[c, e + 2, pl.ds(1, 4)],
            dst_ref=ext.at[c, e, pl.ds(1, 4)],
            send_sem=ts_sem.at[c, e],
            recv_sem=tr_sem.at[c, e],
            device_id=(t_next, h),
            device_id_type=MESH,
        )

    def code_copy(i):
        to = lax.rem(h + i, NH)
        return pltpu.make_async_remote_copy(
            src_ref=msg_ref.at[pl.ds(pl.multiple_of(to * NT, NT), NT)],
            dst_ref=rcodes.at[h],
            send_sem=cs_sem.at[i],
            recv_sem=cr_sem.at[i],
            device_id=(t, to),
            device_id_type=MESH,
        )

    def row_copy(i, s):
        to = lax.rem(h + i, NH)
        return pltpu.make_async_remote_copy(
            src_ref=sbuf.at[to, pl.ds(s * 64, 64)],
            dst_ref=rbuf.at[h, pl.ds(s * 64, 64)],
            send_sem=rs_sem.at[i, s],
            recv_sem=rr_sem.at[i, s],
            device_id=(t, to),
            device_id_type=MESH,
        )

    def spread(c, e):
        for q in range(3):
            for i in range(4):
                x = ext[c, e, i + q]
                ok = None
                if e < 2:
                    ok = t > 0
                if q == 0 and i == 0:
                    ok = (h > 0) if ok is None else jnp.logical_and(ok, h > 0)
                if q == 2 and i == 3:
                    ok = (h < NH - 1) if ok is None else jnp.logical_and(ok, h < NH - 1)
                if ok is not None:
                    x = jnp.where(ok, x, jnp.zeros_like(x))
                cat[e, pl.ds(i * 128, 128), pl.ds(q * C, C)] = x

    def product(c, e, p):
        return jnp.dot(cat[e], wv[c, p], preferred_element_type=F32)

    col = lax.broadcasted_iota(I32, (128, C), 0)

    def finish(f, i, base):
        rows = pl.ds(i * 128, 128)
        left = pltpu.roll(acc[f, rows, pl.ds(0, C)], 1, 0)
        left = jnp.where(col == 0, 0.0, left)
        right = pltpu.roll(acc[f, rows, pl.ds(2 * C, C)], 127, 0)
        right = jnp.where(col == 127, 0.0, right)
        return (base.astype(F32) + ((left + right) + acc[f, rows, pl.ds(C, C)])).astype(BF16)

    for f in (1, 0):
        for i in range(4):
            ext[0, 2 + f, 1 + i] = norm_act(lat_ref[f, i].astype(F32))

    pl.semaphore_wait(barrier, NH + 1)
    for i in range(1, NH):
        code_copy(i).start()
    for e in (3, 2):
        for d in range(2):
            x_copy(0, e, d).start()
    t_copy(0, 1).start()
    t_copy(0, 0).start()
    rcodes[h] = msg_ref[pl.ds(pl.multiple_of(h * NT, NT), NT)]

    def fetch_rows():
        for i in range(1, NH):
            code_copy(i).wait_recv()
        lane_src = lax.shift_right_logical(lax.broadcasted_iota(I32, (NT, 128), 1), 4)
        rowmat = jnp.zeros((NT, 128), I32)
        for s in range(NH):
            rowmat = rowmat + jnp.where(lane_src == s, rcodes[s], 0)
        rowmat = rowmat.astype(F32) - 1.0
        lanes = lax.broadcasted_iota(I32, (128, 128), 1).astype(F32)
        for g in range(NT):
            book_copy(g).wait()
            column = jnp.transpose(jnp.broadcast_to(rowmat[g : g + 1, :], (128, 128)))
            pick = jnp.concatenate(
                [onehot(column - 128.0 * j == lanes) for j in range(K_OWN // 128)], 1
            )
            found = jnp.dot(pick, cbuf[g % 4], preferred_element_type=F32).astype(BF16)
            for s in range(NH):
                sbuf[s, pl.ds(g * CAP, CAP)] = found[s * CAP : (s + 1) * CAP]
            if g + 4 < NT:
                book_copy(g + 4).start()
            if g % 4 == 3:
                for i in range(1, NH):
                    row_copy(i, g // 4).start()
        rbuf[h] = sbuf[h]

    def conv(c, between):
        for e in (3, 2):
            for d in range(2):
                x_copy(c, e, d).wait_recv()
            spread(c, e)
        weights_here(c, 2)
        weights_here(c, 1)
        acc[1] = product(c, 3, 2)
        acc[1] += product(c, 2, 1)
        acc[0] = product(c, 2, 2)
        if between is not None:
            between()
        t_copy(c, 1).wait_recv()
        for d in range(2):
            x_copy(c, 1, d).start()
        for d in range(2):
            x_copy(c, 1, d).wait_recv()
        spread(c, 1)
        weights_here(c, 0)
        acc[1] += product(c, 1, 0)

    def tail(c):
        acc[0] += product(c, 1, 1)
        t_copy(c, 0).wait_recv()
        for d in range(2):
            x_copy(c, 0, d).start()
        for d in range(2):
            x_copy(c, 0, d).wait_recv()
        spread(c, 0)
        acc[0] += product(c, 0, 0)

    def next_frame(f):
        for i in range(4):
            x = finish(f, i, lat_ref[f, i])
            first[f, i] = x
            ext[1, 2 + f, 1 + i] = norm_act(x.astype(F32))
        for d in range(2):
            x_copy(1, 2 + f, d).start()
        t_copy(1, f).start()

    conv(0, fetch_rows)
    next_frame(1)
    tail(0)
    next_frame(0)
    conv(1, None)
    for i in range(4):
        enc_ref[1, i] = finish(1, i, first[1, i])
    tail(1)
    for i in range(4):
        enc_ref[0, i] = finish(0, i, first[0, i])

    for i in range(1, NH):
        for s in range(4):
            row_copy(i, s).wait_recv()
    out = pltpu.make_async_copy(rbuf, rows_ref, out_sem)
    out.start()
    for i in range(1, NH):
        code_copy(i).wait_send()
        for s in range(4):
            row_copy(i, s).wait_send()
    for c in range(2):
        for e in range(4):
            for d in range(2):
                x_copy(c, e, d).wait_send()
        for e in range(2):
            t_copy(c, e).wait_send()
    out.wait()


def conv_and_rows(latents, w1, w2, msg, book):
    vm = pl.BlockSpec(memory_space=pltpu.VMEM)
    hbm = pl.BlockSpec(memory_space=pl.ANY)
    dma = pltpu.SemaphoreType.DMA
    return pl.pallas_call(
        conv_kernel,
        out_shape=(
            jax.ShapeDtypeStruct((2, 4, 128, C), BF16),
            jax.ShapeDtypeStruct((NH, 256, C), BF16),
        ),
        in_specs=[vm, hbm, hbm, vm, hbm],
        out_specs=(vm, hbm),
        scratch_shapes=[
            pltpu.VMEM((2, 3, 3 * C, 3 * C), BF16),
            pltpu.VMEM((2, 4, 6, 128, C), BF16),
            pltpu.VMEM((4, 512, 3 * C), BF16),
            pltpu.VMEM((2, 512, 3 * C), F32),
            pltpu.VMEM((2, 4, 128, C), BF16),
            pltpu.VMEM((NH, NT, 128), I32),
            pltpu.VMEM((4, K_OWN, C), BF16),
            pltpu.VMEM((NH, 256, C), BF16),
            pltpu.VMEM((NH, 256, C), BF16),
            dma((2, 3)),
            dma((2, 4, 2)),
            dma((2, 4, 2)),
            dma((2, 2)),
            dma((2, 2)),
            dma((NH,)),
            dma((NH,)),
            dma((4,)),
            dma((NH, 4)),
            dma((NH, 4)),
            dma,
        ],
        compiler_params=pltpu.CompilerParams(
            collective_id=0, has_side_effects=True, vmem_limit_bytes=VMEM_LIMIT
        ),
        name="conv_and_rows",
    )(latents, w1, w2, msg, book)


def rotate_back(latent, quant, upward):
    lat_norm = jnp.sqrt(jnp.sum(latent * latent, -1, keepdims=True) + 1e-06)
    quant_norm = jnp.sqrt(jnp.sum(quant * quant, -1, keepdims=True) + 1e-06)
    lat_unit = latent / lat_norm
    quant_unit = quant / quant_norm
    cosine = jnp.sum(lat_unit * quant_unit, -1, keepdims=True)
    summed = lat_unit + quant_unit
    turned = upward - summed * (jnp.sum(summed * upward, -1, keepdims=True) / (1.0 + cosine))
    turned = turned + 2.0 * lat_unit * jnp.sum(quant_unit * upward, -1, keepdims=True)
    return quant_norm / lat_norm * turned + 0.5 * (latent - quant)


def grad_kernel(
    enc_ref,
    rows_ref,
    up_ref,
    msg_ref,
    slot_ref,
    grad_ref,
    sums_ref,
    tsend,
    trecv,
    crecv,
    slotcol,
    s_sem,
    r_sem,
    cs_sem,
    cr_sem,
    l_sem,
):
    t = lax.axis_index("tm")
    h = lax.axis_index("height")
    me = t * NH + h
    barrier = pltpu.get_barrier_semaphore()

    def partner(i):
        pt = lax.rem(t + lax.div(i, NH), NT)
        ph = lax.rem(h + lax.rem(i, NH), NH)
        return pt, ph

    @pl.loop(1, OWN)
    def _(i):
        pl.semaphore_signal(barrier, inc=1, device_id=partner(i), device_id_type=MESH)

    lane = lax.broadcasted_iota(I32, (256, 128), 0)
    slots = slot_ref[...]
    enc = enc_ref[...]

    for b in range(SLOTS // 256):
        pick = jnp.concatenate(
            [
                onehot(lane == jnp.broadcast_to(slots[j : j + 1, :], (256, 128)) - b * 256)
                for j in range(8)
            ],
            1,
        )
        placed = jnp.dot(pick, enc, preferred_element_type=F32)
        rows = pl.ds(b * 256, 256)
        tsend[rows] = (rows_ref[rows].astype(F32) - placed).astype(BF16)

    pl.semaphore_wait(barrier, OWN - 1)

    def code_copy(i):
        pt, ph = partner(i)
        return pltpu.make_async_remote_copy(
            src_ref=msg_ref.at[ph * NT + pt],
            dst_ref=crecv.at[me],
            send_sem=cs_sem,
            recv_sem=cr_sem,
            device_id=(pt, ph),
            device_id_type=MESH,
        )

    def term_copy(i):
        pt, ph = partner(i)
        return pltpu.make_async_remote_copy(
            src_ref=tsend.at[pl.ds(pl.multiple_of((ph * NT + pt) * CAP, CAP), CAP)],
            dst_ref=trecv.at[pl.ds(pl.multiple_of(me * CAP, CAP), CAP)],
            send_sem=s_sem,
            recv_sem=r_sem,
            device_id=(pt, ph),
            device_id_type=MESH,
        )

    @pl.loop(1, OWN)
    def _(i):
        code_copy(i).start()
        term_copy(i).start()

    own_codes = pltpu.make_async_copy(msg_ref.at[h * NT + t], crecv.at[me], cr_sem)
    own_codes.start()
    own_terms = pltpu.make_async_copy(
        tsend.at[pl.ds(pl.multiple_of((h * NT + t) * CAP, CAP), CAP)],
        trecv.at[pl.ds(pl.multiple_of(me * CAP, CAP), CAP)],
        r_sem,
    )
    own_terms.start()

    lanes = lax.broadcasted_iota(I32, (128, 128), 1).astype(F32)
    slots_f = slots.astype(F32)
    for j in range(8):
        column = jnp.transpose(jnp.broadcast_to(slots_f[j : j + 1, :], (128, 128)))
        pick = jnp.concatenate(
            [onehot(column - 128.0 * k == lanes) for k in range(SLOTS // 128)], 1
        )
        quant = jnp.dot(pick, rows_ref[...], preferred_element_type=F32)
        cells = pl.ds(j * 128, 128)
        grad_ref[cells] = rotate_back(
            enc_ref[cells].astype(F32), quant, up_ref[cells].astype(F32)
        ).astype(BF16)

    pltpu.make_async_copy(crecv, crecv, cr_sem).wait()
    group = lax.broadcasted_iota(I32, (8, 128), 0)
    mine = lax.shift_right_logical(lax.broadcasted_iota(I32, (8, 128), 1), 4) == group
    row_of = []
    for j in range(SLOTS // 128):
        tile = crecv[pl.ds(j * 8, 8)]
        row_of.append(jnp.sum(jnp.where(mine, tile, 0), axis=0, keepdims=True) - 1)

    pltpu.make_async_copy(trecv, trecv, r_sem).wait()
    for b in range(K_OWN // 256):
        pick = jnp.concatenate(
            [onehot(lane == jnp.broadcast_to(r - b * 256, (256, 128))) for r in row_of], 1
        )
        sums = jnp.dot(pick, trecv[...], preferred_element_type=F32)
        sums_ref[pl.ds(b * 256, 256)] = (2.0 * sums).astype(BF16)

    @pl.loop(1, OWN)
    def _(i):
        code_copy(i).wait_send()
        term_copy(i).wait_send()


def gradients(enc, rows, upstream, msg, slot):
    vm = pl.BlockSpec(memory_space=pltpu.VMEM)
    dma = pltpu.SemaphoreType.DMA
    return pl.pallas_call(
        grad_kernel,
        out_shape=(
            jax.ShapeDtypeStruct((CELLS, C), BF16),
            jax.ShapeDtypeStruct((K_OWN, C), BF16),
        ),
        in_specs=[vm] * 5,
        out_specs=(vm, vm),
        scratch_shapes=[
            pltpu.VMEM((SLOTS, C), BF16),
            pltpu.VMEM((SLOTS, C), BF16),
            pltpu.VMEM((OWN, 128), I32),
            pltpu.VMEM((8, 128), F32),
            dma,
            dma,
            dma,
            dma,
            dma,
        ],
        compiler_params=pltpu.CompilerParams(
            collective_id=1, has_side_effects=True, vmem_limit_bytes=VMEM_LIMIT
        ),
        name="gradients",
    )(enc, rows, upstream, msg, slot)


def on_device(latents, conv_first, conv_second, codebook, codes, upstream):
    msg, slot = make_slots(codes.reshape(8, 128))
    enc, rows = conv_and_rows(latents, conv_first, conv_second, msg, codebook)
    grad, sums = gradients(
        enc.reshape(CELLS, C), rows.reshape(SLOTS, C), upstream.reshape(CELLS, C), msg, slot
    )
    return grad.reshape(upstream.shape), sums


def solution(mesh):
    return jax.shard_map(
        on_device,
        mesh=mesh,
        in_specs=(
            P("tm", "height", None, None),
            P(),
            P(),
            P("height", None),
            P("tm", "height", None),
            P("tm", "height", None, None),
        ),
        out_specs=(P("tm", "height", None, None), P(("height", "tm"), None)),
        check_vma=False,
    )
```

```python
import functools

import jax
import jax.numpy as jnp
from jax import lax
from jax.experimental import pallas as pl
from jax.experimental.pallas import tpu as pltpu
from jax.sharding import PartitionSpec as P

F32 = jnp.float32
BF16 = jnp.bfloat16
I32 = jnp.int32
MESH = pl.DeviceIdType.MESH
C = 256
NT, NH = 16, 8
OWN = NT * NH
CAP = 16
SLOTS = OWN * CAP
K_OWN = 2048
CELLS = 1024
VMEM_LIMIT = 60 * 1024 * 1024


def onehot(cond):
    return jnp.where(cond, 1.0, 0.0).astype(BF16)


def norm_act(values):
    scaled = values * lax.rsqrt(jnp.mean(values * values, -1, keepdims=True) + 1e-06)
    return (scaled / (1.0 + jnp.exp(-scaled))).astype(BF16)


def rotate_back(latent, quant, upward):
    lat_norm = jnp.sqrt(jnp.sum(latent * latent, -1, keepdims=True) + 1e-06)
    quant_norm = jnp.sqrt(jnp.sum(quant * quant, -1, keepdims=True) + 1e-06)
    lat_unit = latent / lat_norm
    quant_unit = quant / quant_norm
    cosine = jnp.sum(lat_unit * quant_unit, -1, keepdims=True)
    summed = lat_unit + quant_unit
    turned = upward - summed * (jnp.sum(summed * upward, -1, keepdims=True) / (1.0 + cosine))
    turned = turned + 2.0 * lat_unit * jnp.sum(quant_unit * upward, -1, keepdims=True)
    return quant_norm / lat_norm * turned + 0.5 * (latent - quant)


def column(row):
    return jnp.transpose(jnp.broadcast_to(row, (128, 128)))


def window_kernel(
    lat_hbm,
    w1_ref,
    w2_ref,
    book_ref,
    codes_ref,
    up_hbm,
    grad_hbm,
    sums_hbm,
    lat,
    up,
    wv,
    ext,
    cat,
    acc,
    first,
    enc,
    msg,
    slot,
    rcodes,
    cbuf,
    sbuf,
    rbuf,
    place,
    placed,
    tsend,
    trecv,
    crecv,
    spread_in,
    sums,
    sums_out,
    grad_out,
    in_sem,
    w_sem,
    xs_sem,
    xr_sem,
    ts_sem,
    tr_sem,
    cs_sem,
    cr_sem,
    cb_sem,
    rs_sem,
    rr_sem,
    ks_sem,
    kr_sem,
    gs_sem,
    gr_sem,
    out_sem,
    know,
):
    t = lax.axis_index("tm")
    h = lax.axis_index("height")
    h_up, h_down = lax.rem(h + NH - 1, NH), lax.rem(h + 1, NH)

    def at_t(by):
        return lax.rem(t + NT + by, NT)

    def at_h(by):
        return lax.rem(h + by, NH)

    barrier = pltpu.get_barrier_semaphore()
    for by in (1, -1):
        pl.semaphore_signal(barrier, inc=1, device_id=(at_t(by), h), device_id_type=MESH)
    for i in range(1, NH):
        pl.semaphore_signal(barrier, inc=1, device_id=(t, at_h(i)), device_id_type=MESH)

    lat_in = [pltpu.make_async_copy(lat_hbm.at[f], lat.at[f], in_sem.at[f]) for f in range(2)]
    up_in = pltpu.make_async_copy(up_hbm, up, in_sem.at[2])
    lat_in[1].start()
    lat_in[0].start()

    def weights_start(c, p):
        w_ref = (w1_ref, w2_ref)[c]
        for q in range(3):
            for r in range(3):
                pltpu.make_async_copy(
                    w_ref.at[p, q, r],
                    wv.at[c, p, pl.ds(q * C, C), pl.ds(r * C, C)],
                    w_sem.at[c, p],
                ).start()

    def weights_here(c, p):
        pltpu.make_async_copy(wv.at[c, p], wv.at[c, p], w_sem.at[c, p]).wait()

    def book_copy(g):
        return pltpu.make_async_copy(
            book_ref.at[pl.ds(g * K_OWN, K_OWN)], cbuf.at[g % 4], cb_sem.at[g % 4]
        )

    def x_copy(c, e, d):
        src, dst, to = ((1, 5, h_up), (4, 0, h_down))[d]
        return pltpu.make_async_remote_copy(
            src_ref=ext.at[c, e, src],
            dst_ref=ext.at[c, e, dst],
            send_sem=xs_sem.at[c, e, d],
            recv_sem=xr_sem.at[c, e, d],
            device_id=(t, to),
            device_id_type=MESH,
        )

    def t_copy(c, e, part):
        rows = (pl.ds(1, 1), pl.ds(4, 1), pl.ds(2, 2))[part]
        return pltpu.make_async_remote_copy(
            src_ref=ext.at[c, e + 2, rows],
            dst_ref=ext.at[c, e, rows],
            send_sem=ts_sem.at[c, e, part],
            recv_sem=tr_sem.at[c, e, part],
            device_id=(at_t(1), h),
            device_id_type=MESH,
        )

    def code_copy(i):
        to = at_h(i)
        return pltpu.make_async_remote_copy(
            src_ref=msg.at[pl.ds(pl.multiple_of(to * NT, NT), NT)],
            dst_ref=rcodes.at[h],
            send_sem=cs_sem.at[i],
            recv_sem=cr_sem.at[i],
            device_id=(t, to),
            device_id_type=MESH,
        )

    def row_copy(i, s):
        to = at_h(i)
        return pltpu.make_async_remote_copy(
            src_ref=sbuf.at[to, pl.ds(s * 64, 64)],
            dst_ref=rbuf.at[h, pl.ds(s * 64, 64)],
            send_sem=rs_sem.at[i, s],
            recv_sem=rr_sem.at[i, s],
            device_id=(t, to),
            device_id_type=MESH,
        )

    def owner(i, dt):
        to_t, to_h = lax.rem(t + dt, NT), at_h(i)
        return to_t, to_h, to_h * NT + to_t

    def key_copy(i, dt):
        to_t, to_h, blk = owner(i, dt)
        return pltpu.make_async_remote_copy(
            src_ref=msg.at[blk],
            dst_ref=crecv.at[i * NT + t],
            send_sem=ks_sem,
            recv_sem=kr_sem,
            device_id=(to_t, to_h),
            device_id_type=MESH,
        )

    def term_copy(i, dt):
        to_t, to_h, blk = owner(i, dt)
        return pltpu.make_async_remote_copy(
            src_ref=tsend.at[pl.ds(pl.multiple_of(blk * CAP, CAP), CAP)],
            dst_ref=trecv.at[pl.ds(pl.multiple_of((i * NT + t) * CAP, CAP), CAP)],
            send_sem=gs_sem,
            recv_sem=gr_sem.at[i // 4],
            device_id=(to_t, to_h),
            device_id_type=MESH,
        )

    def widen(c, e):
        for q in range(3):
            for i in range(4):
                x = ext[c, e, i + q]
                ok = None
                if e < 2:
                    ok = t > 0
                if q == 0 and i == 0:
                    ok = (h > 0) if ok is None else jnp.logical_and(ok, h > 0)
                if q == 2 and i == 3:
                    ok = (h < NH - 1) if ok is None else jnp.logical_and(ok, h < NH - 1)
                if ok is not None:
                    x = jnp.where(ok, x, jnp.zeros_like(x))
                cat[e, pl.ds(i * 128, 128), pl.ds(q * C, C)] = x

    def product(c, e, p):
        return jnp.dot(cat[e], wv[c, p], preferred_element_type=F32)

    col = lax.broadcasted_iota(I32, (128, C), 0)

    def finish(f, i, base):
        rows = pl.ds(i * 128, 128)
        left = pltpu.roll(acc[f, rows, pl.ds(0, C)], 1, 0)
        left = jnp.where(col == 0, 0.0, left)
        right = pltpu.roll(acc[f, rows, pl.ds(2 * C, C)], 127, 0)
        right = jnp.where(col == 127, 0.0, right)
        return (base.astype(F32) + ((left + right) + acc[f, rows, pl.ds(C, C)])).astype(BF16)

    def send_frame(c, f):
        for d in range(2):
            x_copy(c, 2 + f, d).start()
        for part in range(3):
            t_copy(c, f, part).start()

    lane_i = lax.broadcasted_iota(I32, (128, 128), 1)
    lanes = lane_i.astype(F32)

    def make_slots():
        codes = codes_ref[...]
        blk = lax.shift_right_logical(codes, 11)
        off1 = jnp.bitwise_and(codes, K_OWN - 1) + 1
        sub = lax.broadcasted_iota(I32, (OWN, 128), 0)
        ht = jnp.concatenate(
            [onehot(sub == jnp.broadcast_to(blk[j : j + 1, :], (OWN, 128))) for j in range(8)], 1
        )
        upper = onehot(
            lax.broadcasted_iota(I32, (CELLS, CELLS), 0)
            < lax.broadcasted_iota(I32, (CELLS, CELLS), 1)
        )
        before = jnp.dot(ht, upper, preferred_element_type=F32)
        rank_row = jnp.sum(before * ht.astype(F32), axis=0, keepdims=True)
        rank = jnp.concatenate([rank_row[:, j * 128 : (j + 1) * 128] for j in range(8)], 0)
        slot[...] = blk * CAP + rank.astype(I32)
        hi = lax.shift_right_logical(off1, 6).astype(F32)
        lo = jnp.bitwise_and(off1, 63).astype(F32)
        lane16 = jnp.bitwise_and(lane_i, CAP - 1).astype(F32)
        v_hi, v_lo = [], []
        for j in range(8):
            match = column(rank[j : j + 1, :]) == lane16
            v_hi.append(jnp.where(match, column(hi[j : j + 1, :]), 0.0).astype(BF16))
            v_lo.append(jnp.where(match, column(lo[j : j + 1, :]), 0.0).astype(BF16))
        m_hi = jnp.dot(ht, jnp.concatenate(v_hi, 0), preferred_element_type=F32)
        m_lo = jnp.dot(ht, jnp.concatenate(v_lo, 0), preferred_element_type=F32)
        msg[...] = (m_hi * 64.0 + m_lo).astype(I32)

    def asked_rows():
        for i in range(1, NH):
            code_copy(i).wait_recv()
        lane_src = lax.shift_right_logical(lax.broadcasted_iota(I32, (NT, 128), 1), 4)
        rowmat = jnp.zeros((NT, 128), I32)
        for s in range(NH):
            rowmat = rowmat + jnp.where(lane_src == s, rcodes[s], 0)
        return rowmat.astype(F32) - 1.0

    def gather(rowmat, k):
        for g in range(4 * k, 4 * k + 4):
            book_copy(g).wait()
            want = column(rowmat[g : g + 1, :])
            pick = jnp.concatenate(
                [onehot(want - 128.0 * j == lanes) for j in range(K_OWN // 128)], 1
            )
            found = jnp.dot(pick, cbuf[g % 4], preferred_element_type=F32).astype(BF16)
            for s in range(NH):
                sbuf[s, pl.ds(g * CAP, CAP)] = found[s * CAP : (s + 1) * CAP]
            if g + 4 < NT:
                book_copy(g + 4).start()

    def send_rows(k):
        for i in range(1, NH):
            row_copy(i, k).start()

    def tell(r, by):
        for sign in (1, -1):
            pl.semaphore_signal(
                know.at[r], inc=1, device_id=(at_t(sign * by), h), device_id_type=MESH
            )

    lane = lax.broadcasted_iota(I32, (256, 128), 0)

    def make_place():
        @pl.loop(0, SLOTS // 256)
        def _(b):
            rows = pl.ds(pl.multiple_of(b * 256, 256), 256)
            for j in range(8):
                row = slot[pl.ds(j, 1), :] - b * 256
                place[j // 4, rows, pl.ds((j % 4) * 128, 128)] = onehot(
                    lane == jnp.broadcast_to(row, (256, 128))
                )

    def make_spread():
        pltpu.make_async_copy(crecv, crecv, kr_sem).wait()
        group = lax.broadcasted_iota(I32, (8, 128), 0)
        mine = lax.shift_right_logical(lax.broadcasted_iota(I32, (8, 128), 1), 4) == group
        row_of = []
        for j in range(SLOTS // 128):
            tile = crecv[pl.ds(j * 8, 8)]
            row_of.append(jnp.sum(jnp.where(mine, tile, 0), axis=0, keepdims=True) - 1)

        @pl.loop(0, K_OWN // 256)
        def _(b):
            rows = pl.ds(pl.multiple_of(b * 256, 256), 256)
            for j in range(SLOTS // 128):
                spread_in[rows, pl.ds(j * 128, 128)] = onehot(
                    lane == jnp.broadcast_to(row_of[j] - b * 256, (256, 128))
                )

    for f in (1, 0):
        lat_in[f].wait()
        for i in range(4):
            ext[0, 2 + f, 1 + i] = norm_act(lat[f, i].astype(F32))
        if f == 1:
            pl.semaphore_wait(barrier, NH + 1)
        send_frame(0, f)
    tell(0, 1)
    for c in range(2):
        for p in (2, 1, 0):
            weights_start(c, p)
        if c == 0:
            for g in range(4):
                book_copy(g).start()
    up_in.start()

    make_slots()
    for i in range(1, NH):
        code_copy(i).start()
    rcodes[h] = msg[pl.ds(pl.multiple_of(h * NT, NT), NT)]

    def local_part(c):
        for e in (3, 2):
            for d in range(2):
                x_copy(c, e, d).wait_recv()
            widen(c, e)
        if c == 1:
            send_rows(2)
        weights_here(c, 2)
        weights_here(c, 1)
        acc[1] = product(c, 3, 2)
        acc[1] += product(c, 2, 1)
        acc[0] = product(c, 2, 2)

    def earlier_frame(c, e, between, rows_piece):
        for d in range(2):
            t_copy(c, e, d).wait_recv()
            x_copy(c, e, d).start()
        if between is not None:
            between()
        t_copy(c, e, 2).wait_recv()
        for d in range(2):
            x_copy(c, e, d).wait_recv()
        if rows_piece is not None:
            send_rows(rows_piece)
        widen(c, e)
        if e == 1:
            weights_here(c, 0)
            acc[1] += product(c, 1, 0)
        else:
            acc[0] += product(c, 0, 0)

    def next_frame(f):
        for i in range(4):
            x = finish(f, i, lat[f, i])
            first[f, i] = x
            ext[1, 2 + f, 1 + i] = norm_act(x.astype(F32))
        send_frame(1, f)

    local_part(0)
    rowmat = asked_rows()
    gather(rowmat, 0)
    gather(rowmat, 1)
    pl.semaphore_wait(know.at[0], 2)
    tell(1, 2)
    earlier_frame(0, 1, lambda: gather(rowmat, 2), 0)
    next_frame(1)
    acc[0] += product(0, 1, 1)
    pl.semaphore_wait(know.at[1], 2)
    tell(2, 4)
    gather(rowmat, 3)
    rbuf[h] = sbuf[h]
    earlier_frame(0, 0, None, 1)
    next_frame(0)

    pl.semaphore_wait(know.at[2], 2)
    for i in range(1, NH):
        pl.semaphore_signal(know.at[3], inc=1, device_id=(t, at_h(i)), device_id_type=MESH)
    make_place()
    local_part(1)

    def send_keys():
        pl.semaphore_wait(know.at[3], NH - 1)
        for i in range(NH):

            @pl.loop(1 if i == 0 else 0, NT)
            def _(dt):
                key_copy(i, dt).start()

        pltpu.make_async_copy(msg.at[h * NT + t], crecv.at[t], kr_sem).start()

    send_keys()
    earlier_frame(1, 1, None, 3)
    for i in range(4):
        enc[1, pl.ds(i * 128, 128)] = finish(1, i, first[1, i])
    acc[0] += product(1, 1, 1)
    placed[...] = jnp.dot(place[1], enc[1], preferred_element_type=F32)
    make_spread()
    earlier_frame(1, 0, None, None)
    for i in range(4):
        enc[0, pl.ds(i * 128, 128)] = finish(0, i, first[0, i])

    for s in range(4):
        for i in range(1, NH):
            row_copy(i, s).wait_recv()

    for i in range(NH):
        to_h = at_h(i)
        rows = pl.ds(pl.multiple_of(to_h * 256, 256), 256)
        total = placed[rows] + jnp.dot(place[0, rows], enc[0], preferred_element_type=F32)
        tsend[rows] = (rbuf[to_h].astype(F32) - total).astype(BF16)

        @pl.loop(1 if i == 0 else 0, NT)
        def _(dt):
            term_copy(i, dt).start()

        if i == 0:
            pltpu.make_async_copy(
                tsend.at[pl.ds(pl.multiple_of((h * NT + t) * CAP, CAP), CAP)],
                trecv.at[pl.ds(pl.multiple_of(t * CAP, CAP), CAP)],
                gr_sem.at[0],
            ).start()

    up_in.wait()
    rows_all = rbuf[...].reshape(SLOTS, C)
    for j in range(8):
        want = column(slot[pl.ds(j, 1), :].astype(F32))
        pick = jnp.concatenate([onehot(want - 128.0 * k == lanes) for k in range(SLOTS // 128)], 1)
        quant = jnp.dot(pick, rows_all, preferred_element_type=F32)
        cells = pl.ds((j % 4) * 128, 128)
        grad_out[pl.ds(j * 128, 128)] = rotate_back(
            enc[j // 4, cells].astype(F32), quant, up[pl.ds(j * 128, 128)].astype(F32)
        ).astype(BF16)
    grad_done = pltpu.make_async_copy(grad_out, grad_hbm, out_sem.at[0])
    grad_done.start()

    half = SLOTS // 2
    low, high = pl.ds(0, half), pl.ds(half, half)
    pltpu.make_async_copy(trecv.at[low], trecv.at[low], gr_sem.at[0]).wait()
    sums[...] = jnp.dot(spread_in[:, low], trecv[low], preferred_element_type=F32)
    pltpu.make_async_copy(trecv.at[high], trecv.at[high], gr_sem.at[1]).wait()
    done = []
    for b in range(4):
        rows = pl.ds(b * 512, 512)
        total = sums[rows] + jnp.dot(
            spread_in[rows, high], trecv[high], preferred_element_type=F32
        )
        sums_out[rows] = (2.0 * total).astype(BF16)
        copy = pltpu.make_async_copy(sums_out.at[rows], sums_hbm.at[rows], out_sem.at[1 + b])
        copy.start()
        done.append(copy)

    for i in range(1, NH):
        code_copy(i).wait_send()
        for s in range(4):
            row_copy(i, s).wait_send()
    for c in range(2):
        for e in range(4):
            for d in range(2):
                x_copy(c, e, d).wait_send()
        for e in range(2):
            for part in range(3):
                t_copy(c, e, part).wait_send()
    sent = pl.ds(0, SLOTS - CAP)
    pltpu.make_async_copy(tsend.at[sent], tsend.at[sent], gs_sem).wait()
    sent = pl.ds(0, OWN - 1)
    pltpu.make_async_copy(crecv.at[sent], crecv.at[sent], ks_sem).wait()
    grad_done.wait()
    for copy in done:
        copy.wait()


def window(latents, w1, w2, book, codes, upstream):
    vm = pl.BlockSpec(memory_space=pltpu.VMEM)
    hbm = pl.BlockSpec(memory_space=pl.ANY)
    dma = pltpu.SemaphoreType.DMA
    return pl.pallas_call(
        window_kernel,
        out_shape=(
            jax.ShapeDtypeStruct((CELLS, C), BF16),
            jax.ShapeDtypeStruct((K_OWN, C), BF16),
        ),
        in_specs=[hbm, hbm, hbm, hbm, vm, hbm],
        out_specs=(hbm, hbm),
        scratch_shapes=[
            pltpu.VMEM((2, 4, 128, C), BF16),
            pltpu.VMEM((CELLS, C), BF16),
            pltpu.VMEM((2, 3, 3 * C, 3 * C), BF16),
            pltpu.VMEM((2, 4, 6, 128, C), BF16),
            pltpu.VMEM((4, 512, 3 * C), BF16),
            pltpu.VMEM((2, 512, 3 * C), F32),
            pltpu.VMEM((2, 4, 128, C), BF16),
            pltpu.VMEM((2, 512, C), BF16),
            pltpu.VMEM((OWN, 128), I32),
            pltpu.VMEM((8, 128), I32),
            pltpu.VMEM((NH, NT, 128), I32),
            pltpu.VMEM((4, K_OWN, C), BF16),
            pltpu.VMEM((NH, 256, C), BF16),
            pltpu.VMEM((NH, 256, C), BF16),
            pltpu.VMEM((2, SLOTS, 512), BF16),
            pltpu.VMEM((SLOTS, C), F32),
            pltpu.VMEM((SLOTS, C), BF16),
            pltpu.VMEM((SLOTS, C), BF16),
            pltpu.VMEM((OWN, 128), I32),
            pltpu.VMEM((K_OWN, SLOTS), BF16),
            pltpu.VMEM((K_OWN, C), F32),
            pltpu.VMEM((K_OWN, C), BF16),
            pltpu.VMEM((CELLS, C), BF16),
            dma((3,)),
            dma((2, 3)),
            dma((2, 4, 2)),
            dma((2, 4, 2)),
            dma((2, 2, 3)),
            dma((2, 2, 3)),
            dma((NH,)),
            dma((NH,)),
            dma((4,)),
            dma((NH, 4)),
            dma((NH, 4)),
            dma,
            dma,
            dma,
            dma((2,)),
            dma((5,)),
            pltpu.SemaphoreType.REGULAR((4,)),
        ],
        compiler_params=pltpu.CompilerParams(
            collective_id=0, has_side_effects=True, vmem_limit_bytes=VMEM_LIMIT
        ),
        name="window",
    )(latents, w1, w2, book, codes, upstream)


def hand_kernel(grad_in, sums_in, grad_ref, sums_ref, grad_buf, sums_buf, in_sem, out_sem):
    pieces = [(grad_in, grad_buf, grad_ref, 0), (grad_in, grad_buf, grad_ref, 1)] + [
        (sums_in, sums_buf, sums_ref, k) for k in range(4)
    ]
    ins, outs = [], []
    for n, (src, buf, dst, k) in enumerate(pieces):
        rows = pl.ds(k * 512, 512)
        ins.append(pltpu.make_async_copy(src.at[rows], buf.at[rows], in_sem.at[n]))
        outs.append(pltpu.make_async_copy(buf.at[rows], dst.at[rows], out_sem.at[n]))
        ins[-1].start()
    for n in range(len(pieces)):
        ins[n].wait()
        outs[n].start()
    for n in range(len(pieces)):
        outs[n].wait()


def hand_over(grad, sums):
    hbm = pl.BlockSpec(memory_space=pl.ANY)
    dma = pltpu.SemaphoreType.DMA
    return pl.pallas_call(
        hand_kernel,
        out_shape=(
            jax.ShapeDtypeStruct((CELLS, C), BF16),
            jax.ShapeDtypeStruct((K_OWN, C), BF16),
        ),
        in_specs=[hbm, hbm],
        out_specs=(hbm, hbm),
        scratch_shapes=[
            pltpu.VMEM((CELLS, C), BF16),
            pltpu.VMEM((K_OWN, C), BF16),
            dma((6,)),
            dma((6,)),
        ],
        name="hand_over",
    )(grad, sums)


def on_device(latents, conv_first, conv_second, codebook, codes, upstream):
    grad, sums = window(
        latents,
        conv_first,
        conv_second,
        codebook,
        codes.reshape(8, 128),
        upstream.reshape(CELLS, C),
    )
    grad, sums = hand_over(grad, sums)
    return grad.reshape(upstream.shape), sums


def solution(mesh):
    return jax.shard_map(
        on_device,
        mesh=mesh,
        in_specs=(
            P("tm", "height", None, None),
            P(),
            P(),
            P("height", None),
            P("tm", "height", None),
            P("tm", "height", None, None),
        ),
        out_specs=(P("tm", "height", None, None), P(("height", "tm"), None)),
        check_vma=False,
    )
```

```python
import contextlib

import jax
import jax.numpy as jnp
from jax import lax
from jax.experimental import pallas as pl
from jax.experimental.pallas import tpu as pltpu
from jax.sharding import PartitionSpec as P

F32 = jnp.float32
BF16 = jnp.bfloat16
I32 = jnp.int32
MESH = pl.DeviceIdType.MESH
C = 256
NT, NH = 16, 8
OWN = NT * NH
CAP = 16
SLOTS = OWN * CAP
K_OWN = 2048
CELLS = 1024
VMEM_LIMIT = 60 * 1024 * 1024
STEPS = ((2, 0), (2, 1), (1, 0), (1, 1), (3, 0), (3, 1), (0, 1), (0, 0))


def scope(name):
    return contextlib.nullcontext()


def onehot(cond):
    return jnp.where(cond, 1.0, 0.0).astype(BF16)


def norm_act(values):
    scaled = values * lax.rsqrt(jnp.mean(values * values, -1, keepdims=True) + 1e-06)
    return (scaled / (1.0 + jnp.exp(-scaled))).astype(BF16)


def rotate_back(latent, quant, upward):
    lat_norm = jnp.sqrt(jnp.sum(latent * latent, -1, keepdims=True) + 1e-06)
    quant_norm = jnp.sqrt(jnp.sum(quant * quant, -1, keepdims=True) + 1e-06)
    lat_unit = latent / lat_norm
    quant_unit = quant / quant_norm
    cosine = jnp.sum(lat_unit * quant_unit, -1, keepdims=True)
    summed = lat_unit + quant_unit
    turned = upward - summed * (jnp.sum(summed * upward, -1, keepdims=True) / (1.0 + cosine))
    turned = turned + 2.0 * lat_unit * jnp.sum(quant_unit * upward, -1, keepdims=True)
    return quant_norm / lat_norm * turned + 0.5 * (latent - quant)


def masked(low, high):
    tiles = low.reshape(low.shape[0] // 16, 16, 128)
    return (tiles * jnp.broadcast_to(high, (16, 128)).astype(BF16)[None]).reshape(low.shape)


def column(row):
    return jnp.transpose(jnp.broadcast_to(row, (128, 128)))


def window_kernel(
    lat_hbm,
    w1_ref,
    w2_ref,
    book_ref,
    codes_ref,
    up_hbm,
    grad_hbm,
    sums_hbm,
    lat,
    up,
    wv,
    ext,
    cat,
    acc,
    first,
    enc,
    msg,
    slot,
    rcodes,
    cbuf,
    sbuf,
    rbuf,
    place,
    placed,
    tsend,
    trecv,
    crecv,
    spread_in,
    sums,
    sums_out,
    grad_out,
    in_sem,
    w_sem,
    xs_sem,
    xr_sem,
    ts_sem,
    tr_sem,
    cs_sem,
    cr_sem,
    cb_sem,
    rs_sem,
    rr_sem,
    ks_sem,
    kr_sem,
    gs_sem,
    gr_sem,
    out_sem,
    know,
):
    t = lax.axis_index("tm")
    h = lax.axis_index("height")
    h_up, h_down = lax.rem(h + NH - 1, NH), lax.rem(h + 1, NH)

    def at_t(by):
        return lax.rem(t + NT + by, NT)

    def at_h(by):
        return lax.rem(h + by, NH)

    barrier = pltpu.get_barrier_semaphore()
    for by in (1, -1):
        pl.semaphore_signal(barrier, inc=1, device_id=(at_t(by), h), device_id_type=MESH)
    for i in range(1, NH):
        pl.semaphore_signal(barrier, inc=1, device_id=(t, at_h(i)), device_id_type=MESH)

    lat_in = [pltpu.make_async_copy(lat_hbm.at[f], lat.at[f], in_sem.at[f]) for f in range(2)]
    up_in = pltpu.make_async_copy(up_hbm, up, in_sem.at[2])
    lat_in[1].start()
    lat_in[0].start()

    def weights_start(c, p):
        w_ref = (w1_ref, w2_ref)[c]
        for q in range(3):
            for r in range(3):
                pltpu.make_async_copy(
                    w_ref.at[p, q, r],
                    wv.at[c, p, pl.ds(q * C, C), pl.ds(r * C, C)],
                    w_sem.at[c, p],
                ).start()

    for p in (2, 1, 0):
        weights_start(0, p)

    def weights_here(c, p):
        pltpu.make_async_copy(wv.at[c, p], wv.at[c, p], w_sem.at[c, p]).wait()

    def book_copy(g):
        return pltpu.make_async_copy(
            book_ref.at[pl.ds(g * K_OWN, K_OWN)], cbuf.at[g % 4], cb_sem.at[g % 4]
        )

    def x_copy(c, e, d):
        src, dst, to = ((1, 5, h_up), (4, 0, h_down))[d]
        return pltpu.make_async_remote_copy(
            src_ref=ext.at[c, e, src],
            dst_ref=ext.at[c, e, dst],
            send_sem=xs_sem.at[c, e, d],
            recv_sem=xr_sem.at[c, e, d],
            device_id=(t, to),
            device_id_type=MESH,
        )

    def t_copy(c, e, part):
        rows = (pl.ds(1, 1), pl.ds(4, 1), pl.ds(2, 2))[part]
        return pltpu.make_async_remote_copy(
            src_ref=ext.at[c, e + 2, rows],
            dst_ref=ext.at[c, e, rows],
            send_sem=ts_sem.at[c, e, part],
            recv_sem=tr_sem.at[c, e, part],
            device_id=(at_t(1), h),
            device_id_type=MESH,
        )

    def column_at(i, sign):
        dx, dc = STEPS[i]
        x = lax.rem(lax.div(h, 2) + 4 + sign * dx, 4)
        return x * 2 + lax.rem(lax.rem(h, 2) + dc, 2)

    def code_copy(i):
        to = column_at(i, 1)
        return pltpu.make_async_remote_copy(
            src_ref=msg.at[pl.ds(pl.multiple_of(to * NT, NT), NT)],
            dst_ref=rcodes.at[:, h],
            send_sem=cs_sem.at[i],
            recv_sem=cr_sem.at[i],
            device_id=(t, to),
            device_id_type=MESH,
        )

    def row_copy(i, s):
        to = column_at(i, 1)
        return pltpu.make_async_remote_copy(
            src_ref=sbuf.at[to, pl.ds(s * 64, 64)],
            dst_ref=rbuf.at[h, pl.ds(s * 64, 64)],
            send_sem=rs_sem.at[i, s],
            recv_sem=rr_sem.at[i, s],
            device_id=(t, to),
            device_id_type=MESH,
        )

    def key_copy(dt):
        to = lax.rem(t + dt, NT)
        return pltpu.make_async_remote_copy(
            src_ref=rcodes.at[to],
            dst_ref=crecv.at[:, t],
            send_sem=ks_sem.at[dt],
            recv_sem=kr_sem.at[dt],
            device_id=(to, h),
            device_id_type=MESH,
        )

    def term_copy(i, k):
        def far(n):
            return lax.rem(2 + 3 * n + lax.div(n, 2) * (3 + 2 * lax.rem(n, 2)), 4)

        y = lax.rem(lax.rem(t, 4) + far(lax.rem(k, 4)), 4)
        z = lax.rem(lax.div(t, 4) + far(lax.div(k, 4)), 4)
        to_t, to_h = z * 4 + y, column_at(i, 1)
        return pltpu.make_async_remote_copy(
            src_ref=tsend.at[pl.ds(pl.multiple_of((to_h * NT + to_t) * CAP, CAP), CAP)],
            dst_ref=trecv.at[pl.ds(pl.multiple_of((i * NT + t) * CAP, CAP), CAP)],
            send_sem=gs_sem,
            recv_sem=gr_sem.at[i // 2],
            device_id=(to_t, to_h),
            device_id_type=MESH,
        )

    def widen(c, e):
        for q in range(3):
            for i in range(4):
                x = ext[c, e, i + q]
                ok = None
                if e < 2:
                    ok = t > 0
                if q == 0 and i == 0:
                    ok = (h > 0) if ok is None else jnp.logical_and(ok, h > 0)
                if q == 2 and i == 3:
                    ok = (h < NH - 1) if ok is None else jnp.logical_and(ok, h < NH - 1)
                if ok is not None:
                    x = jnp.where(ok, x, jnp.zeros_like(x))
                cat[e, pl.ds(i * 128, 128), pl.ds(q * C, C)] = x

    def product(c, e, p):
        return jnp.dot(cat[e], wv[c, p], preferred_element_type=F32)

    col = lax.broadcasted_iota(I32, (128, C), 0)

    def finish(f, i, base):
        rows = pl.ds(i * 128, 128)
        left = pltpu.roll(acc[f, rows, pl.ds(0, C)], 1, 0)
        left = jnp.where(col == 0, 0.0, left)
        right = pltpu.roll(acc[f, rows, pl.ds(2 * C, C)], 127, 0)
        right = jnp.where(col == 127, 0.0, right)
        return (base.astype(F32) + ((left + right) + acc[f, rows, pl.ds(C, C)])).astype(BF16)

    def send_frame(c, f):
        for d in range(2):
            x_copy(c, 2 + f, d).start()
        for part in range(3):
            t_copy(c, f, part).start()

    lane_i = lax.broadcasted_iota(I32, (128, 128), 1)

    def make_slots():
        codes = codes_ref[...]
        blk = lax.shift_right_logical(codes, 11)
        off1 = jnp.bitwise_and(codes, K_OWN - 1) + 1
        sub = lax.broadcasted_iota(I32, (OWN, 128), 0)
        ht = jnp.concatenate(
            [onehot(sub == jnp.broadcast_to(blk[j : j + 1, :], (OWN, 128))) for j in range(8)], 1
        )
        upper = onehot(
            lax.broadcasted_iota(I32, (CELLS, CELLS), 0)
            < lax.broadcasted_iota(I32, (CELLS, CELLS), 1)
        )
        before = jnp.dot(ht, upper, preferred_element_type=F32)
        rank_row = jnp.sum(before * ht.astype(F32), axis=0, keepdims=True)
        rank = jnp.concatenate([rank_row[:, j * 128 : (j + 1) * 128] for j in range(8)], 0)
        slot[...] = blk * CAP + rank.astype(I32)
        hi = lax.shift_right_logical(off1, 6).astype(F32)
        lo = jnp.bitwise_and(off1, 63).astype(F32)
        lane16 = jnp.bitwise_and(lane_i, CAP - 1).astype(F32)
        v_hi, v_lo = [], []
        for j in range(8):
            match = column(rank[j : j + 1, :]) == lane16
            v_hi.append(jnp.where(match, column(hi[j : j + 1, :]), 0.0).astype(BF16))
            v_lo.append(jnp.where(match, column(lo[j : j + 1, :]), 0.0).astype(BF16))
        m_hi = jnp.dot(ht, jnp.concatenate(v_hi, 0), preferred_element_type=F32)
        m_lo = jnp.dot(ht, jnp.concatenate(v_lo, 0), preferred_element_type=F32)
        msg[...] = (m_hi * 64.0 + m_lo).astype(I32)

    group8 = lax.broadcasted_iota(I32, (8, 128), 0)
    mine = lax.shift_right_logical(lax.broadcasted_iota(I32, (8, 128), 1), 4) == group8

    def key_row(tile):
        return jnp.sum(jnp.where(mine, tile, 0), axis=0, keepdims=True) - 1

    def pick_rows(want, tiles):
        want = want.astype(I32)
        low = onehot(jnp.bitwise_and(want, 127) == lane_i)
        high = lax.shift_right_arithmetic(want, 7).astype(F32).astype(BF16)
        return jnp.concatenate(
            [jnp.where(high == float(j), low, jnp.zeros_like(low)) for j in range(tiles)], 1
        )

    def gather(k):
        for g in range(4 * k, 4 * k + 4):
            book_copy(g).wait()
            pick = pick_rows(column(key_row(rcodes[g]).astype(F32)), K_OWN // 128)
            found = jnp.dot(pick, cbuf[g % 4], preferred_element_type=F32).astype(BF16)
            for s in range(NH):
                sbuf[s, pl.ds(g * CAP, CAP)] = found[s * CAP : (s + 1) * CAP]
            if g + 4 < NT:
                book_copy(g + 4).start()

    def send_rows(k):
        for i in range(NH - 1):
            row_copy(i, k).start()

    def tell(r, by):
        for sign in (1, -1):
            pl.semaphore_signal(
                know.at[r], inc=1, device_id=(at_t(sign * by), h), device_id_type=MESH
            )

    lane = lax.broadcasted_iota(I32, (256, 128), 0)

    def lay_one_hot(ref, lanes_at, row):
        low = onehot(lane == jnp.broadcast_to(jnp.bitwise_and(row, 255), (256, 128)))
        high = lax.shift_right_arithmetic(row, 8)
        for b in range(8):
            ref[pl.ds(b * 256, 256), lanes_at] = masked(low, jnp.where(high == b, 1.0, 0.0))

    def make_place():
        for j in range(8):
            lay_one_hot(place.at[j // 4], pl.ds((j % 4) * 128, 128), slot[pl.ds(j, 1), :])

    def make_spread():
        for dt in range(1, NT):
            key_copy(dt).wait_recv()
        own_keys.wait()
        for i in range(NH):
            keys = crecv[column_at(i, -1)]
            for half in range(2):
                row = key_row(keys[half * 8 : half * 8 + 8])
                lay_one_hot(spread_in, pl.ds(i * 256 + half * 128, 128), row)

    def next_frame(f):
        with scope("next"):
            for i in range(4):
                x = finish(f, i, lat[f, i])
                first[f, i] = x
                ext[1, 2 + f, 1 + i] = norm_act(x.astype(F32))
        send_frame(1, f)

    def rows_of(c, e):
        with scope("wait_x"):
            for d in range(2):
                x_copy(c, e, d).wait_recv()
        with scope("widen"):
            widen(c, e)

    def forward(c, e):
        with scope(f"wait_edge{c}{e}"):
            for d in range(2):
                t_copy(c, e, d).wait_recv()
                x_copy(c, e, d).start()

    def earlier_frame(c, e):
        with scope(f"wait_mid{c}{e}"):
            t_copy(c, e, 2).wait_recv()
        with scope(f"wait_fwd{c}{e}"):
            for d in range(2):
                x_copy(c, e, d).wait_recv()

    for f in (1, 0):
        with scope("latin"):
            lat_in[f].wait()
        with scope("act"):
            for i in range(4):
                ext[0, 2 + f, 1 + i] = norm_act(lat[f, i].astype(F32))
        if f == 1:
            with scope("barrier"):
                pl.semaphore_wait(barrier, NH + 1)
        send_frame(0, f)
    tell(0, 1)
    for g in range(4):
        book_copy(g).start()
    up_in.start()

    with scope("slots"):
        make_slots()
    for i in range(NH - 1):
        code_copy(i).start()
    rcodes[:, h] = msg[pl.ds(pl.multiple_of(h * NT, NT), NT)]

    rows_of(0, 3)
    weights_here(0, 2)
    with scope("mm"):
        acc[1] = product(0, 3, 2)
    rows_of(0, 2)
    forward(0, 1)
    weights_here(0, 1)
    with scope("mm"):
        acc[1] += product(0, 2, 1)
        acc[0] = product(0, 2, 2)
    for p in (2, 1, 0):
        weights_start(1, p)
    with scope("asked"):
        for i in range(NH - 1):
            code_copy(i).wait_recv()
    with scope("gather"):
        gather(0)
    with scope("know"):
        pl.semaphore_wait(know.at[0], 2)
    tell(1, 2)
    earlier_frame(0, 1)
    send_rows(0)
    weights_here(0, 0)
    with scope("mm"):
        widen(0, 1)
        acc[1] += product(0, 1, 0)
    next_frame(1)
    with scope("mm"):
        acc[0] += product(0, 1, 1)
    forward(0, 0)
    with scope("know"):
        pl.semaphore_wait(know.at[1], 2)
    tell(2, 4)
    with scope("gather"):
        gather(1)
        gather(2)
    earlier_frame(0, 0)
    send_rows(1)
    with scope("mm"):
        widen(0, 0)
        acc[0] += product(0, 0, 0)
    next_frame(0)

    with scope("know"):
        pl.semaphore_wait(know.at[2], 2)
    for i in range(1, NH):
        pl.semaphore_signal(know.at[3], inc=1, device_id=(t, at_h(i)), device_id_type=MESH)
    for dt in range(1, NT):
        key_copy(dt).start()
    own_keys = pltpu.make_async_copy(rcodes.at[t], crecv.at[:, t], kr_sem.at[0])
    own_keys.start()
    rows_of(1, 3)
    weights_here(1, 2)
    with scope("mm"):
        acc[1] = product(1, 3, 2)
    forward(1, 1)
    with scope("gather"):
        gather(3)
    rbuf[h] = sbuf[h]
    with scope("place"):
        make_place()
    rows_of(1, 2)
    send_rows(2)
    weights_here(1, 1)
    with scope("mm"):
        acc[1] += product(1, 2, 1)
        acc[0] = product(1, 2, 2)
    earlier_frame(1, 1)
    send_rows(3)
    weights_here(1, 0)
    with scope("mm"):
        widen(1, 1)
        acc[1] += product(1, 1, 0)
    for i in range(4):
        enc[1, pl.ds(i * 128, 128)] = finish(1, i, first[1, i])
    with scope("mm"):
        acc[0] += product(1, 1, 1)
    forward(1, 0)
    with scope("placed"):
        placed[...] = jnp.dot(place[1], enc[1], preferred_element_type=F32)
    with scope("spread"):
        make_spread()
    with scope("know"):
        pl.semaphore_wait(know.at[3], NH - 1)
    earlier_frame(1, 0)
    with scope("mm"):
        widen(1, 0)
        acc[0] += product(1, 0, 0)
    for i in range(4):
        enc[0, pl.ds(i * 128, 128)] = finish(0, i, first[0, i])

    with scope("wait_rows"):
        for s in range(4):
            for i in range(NH - 1):
                row_copy(i, s).wait_recv()

    for chip in range(4):
        to_x = lax.rem(lax.div(h, 2) + STEPS[2 * chip][0], 4)
        rows = pl.ds(pl.multiple_of(to_x * 512, 512), 512)
        with scope("terms"):
            total = placed[rows] + jnp.dot(place[0, rows], enc[0], preferred_element_type=F32)
            pair = rbuf[pl.ds(to_x * 2, 2)].reshape(512, C)
            tsend[rows] = (pair.astype(F32) - total).astype(BF16)

        @pl.loop(0, NT)
        def _(k):
            term_copy(2 * chip, k).start()
            if chip < 3:
                term_copy(2 * chip + 1, k).start()
            else:

                @pl.when(k < NT - 1)
                def _():
                    term_copy(NH - 1, k).start()

    pltpu.make_async_copy(
        tsend.at[pl.ds(pl.multiple_of((h * NT + t) * CAP, CAP), CAP)],
        trecv.at[pl.ds(pl.multiple_of(((NH - 1) * NT + t) * CAP, CAP), CAP)],
        gr_sem.at[3],
    ).start()

    with scope("grad"):
        up_in.wait()
        rows_all = rbuf[...].reshape(SLOTS, C)
        for j in range(8):
            pick = pick_rows(column(slot[pl.ds(j, 1), :].astype(F32)), SLOTS // 128)
            quant = jnp.dot(pick, rows_all, preferred_element_type=F32)
            cells = pl.ds((j % 4) * 128, 128)
            grad_out[pl.ds(j * 128, 128)] = rotate_back(
                enc[j // 4, cells].astype(F32), quant, up[pl.ds(j * 128, 128)].astype(F32)
            ).astype(BF16)
    grad_done = pltpu.make_async_copy(grad_out, grad_hbm, out_sem.at[0])
    grad_done.start()

    for i in range(NH - 1):
        code_copy(i).wait_send()
        for s in range(4):
            row_copy(i, s).wait_send()
    for dt in range(1, NT):
        key_copy(dt).wait_send()
    for c in range(2):
        for e in range(4):
            for d in range(2):
                x_copy(c, e, d).wait_send()
        for e in range(2):
            for part in range(3):
                t_copy(c, e, part).wait_send()

    def arrived(chip):
        part = pl.ds(chip * 512, 512)
        with scope(f"wait_terms{chip}"):
            pltpu.make_async_copy(trecv.at[part], trecv.at[part], gr_sem.at[chip]).wait()

    def summed(rows, part):
        return jnp.dot(spread_in[rows, part], trecv[part], preferred_element_type=F32)

    everything = pl.ds(0, K_OWN)
    arrived(0)
    arrived(1)
    with scope("sums"):
        sums[...] = summed(everything, pl.ds(0, 1024))
    arrived(2)
    with scope("sums"):
        sums[...] += summed(everything, pl.ds(1024, 512))
    sent = pl.ds(0, SLOTS - CAP)
    with scope("sent"):
        pltpu.make_async_copy(tsend.at[sent], tsend.at[sent], gs_sem).wait()
    arrived(3)
    done = []
    with scope("sums"):
        for b in range(2):
            rows = pl.ds(b * 1024, 1024)
            total = sums[rows] + summed(rows, pl.ds(1536, 512))
            sums_out[rows] = (2.0 * total).astype(BF16)
            copy = pltpu.make_async_copy(sums_out.at[rows], sums_hbm.at[rows], out_sem.at[1 + b])
            copy.start()
            done.append(copy)
    grad_done.wait()
    for copy in done:
        copy.wait()


def window(latents, w1, w2, book, codes, upstream):
    vm = pl.BlockSpec(memory_space=pltpu.VMEM)
    hbm = pl.BlockSpec(memory_space=pl.ANY)
    dma = pltpu.SemaphoreType.DMA
    return pl.pallas_call(
        window_kernel,
        out_shape=(
            jax.ShapeDtypeStruct((CELLS, C), BF16),
            jax.ShapeDtypeStruct((K_OWN, C), BF16),
        ),
        in_specs=[hbm, hbm, hbm, hbm, vm, hbm],
        out_specs=(hbm, hbm),
        scratch_shapes=[
            pltpu.VMEM((2, 4, 128, C), BF16),
            pltpu.VMEM((CELLS, C), BF16),
            pltpu.VMEM((2, 3, 3 * C, 3 * C), BF16),
            pltpu.VMEM((2, 4, 6, 128, C), BF16),
            pltpu.VMEM((4, 512, 3 * C), BF16),
            pltpu.VMEM((2, 512, 3 * C), F32),
            pltpu.VMEM((2, 4, 128, C), BF16),
            pltpu.VMEM((2, 512, C), BF16),
            pltpu.VMEM((OWN, 128), I32),
            pltpu.VMEM((8, 128), I32),
            pltpu.VMEM((NT, NH, 128), I32),
            pltpu.VMEM((4, K_OWN, C), BF16),
            pltpu.VMEM((NH, 256, C), BF16),
            pltpu.VMEM((NH, 256, C), BF16),
            pltpu.VMEM((2, SLOTS, 512), BF16),
            pltpu.VMEM((SLOTS, C), F32),
            pltpu.VMEM((SLOTS, C), BF16),
            pltpu.VMEM((SLOTS, C), BF16),
            pltpu.VMEM((NH, NT, 128), I32),
            pltpu.VMEM((K_OWN, SLOTS), BF16),
            pltpu.VMEM((K_OWN, C), F32),
            pltpu.VMEM((K_OWN, C), BF16),
            pltpu.VMEM((CELLS, C), BF16),
            dma((3,)),
            dma((2, 3)),
            dma((2, 4, 2)),
            dma((2, 4, 2)),
            dma((2, 2, 3)),
            dma((2, 2, 3)),
            dma((NH,)),
            dma((NH,)),
            dma((4,)),
            dma((NH, 4)),
            dma((NH, 4)),
            dma((NT,)),
            dma((NT,)),
            dma,
            dma((4,)),
            dma((3,)),
            pltpu.SemaphoreType.REGULAR((4,)),
        ],
        compiler_params=pltpu.CompilerParams(
            collective_id=0, has_side_effects=True, vmem_limit_bytes=VMEM_LIMIT
        ),
        name="window",
    )(latents, w1, w2, book, codes, upstream)


def hand_kernel(grad_in, sums_in, grad_ref, sums_ref, grad_buf, sums_buf, in_sem, out_sem):
    pieces = [(grad_in, grad_buf, grad_ref, 0), (grad_in, grad_buf, grad_ref, 1)] + [
        (sums_in, sums_buf, sums_ref, k) for k in range(4)
    ]
    ins, outs = [], []
    for n, (src, buf, dst, k) in enumerate(pieces):
        rows = pl.ds(k * 512, 512)
        ins.append(pltpu.make_async_copy(src.at[rows], buf.at[rows], in_sem.at[n]))
        outs.append(pltpu.make_async_copy(buf.at[rows], dst.at[rows], out_sem.at[n]))
        ins[-1].start()
    for n in range(len(pieces)):
        ins[n].wait()
        outs[n].start()
    for n in range(len(pieces)):
        outs[n].wait()


def hand_over(grad, sums):
    hbm = pl.BlockSpec(memory_space=pl.ANY)
    dma = pltpu.SemaphoreType.DMA
    return pl.pallas_call(
        hand_kernel,
        out_shape=(
            jax.ShapeDtypeStruct((CELLS, C), BF16),
            jax.ShapeDtypeStruct((K_OWN, C), BF16),
        ),
        in_specs=[hbm, hbm],
        out_specs=(hbm, hbm),
        scratch_shapes=[
            pltpu.VMEM((CELLS, C), BF16),
            pltpu.VMEM((K_OWN, C), BF16),
            dma((6,)),
            dma((6,)),
        ],
        name="hand_over",
    )(grad, sums)


def on_device(latents, conv_first, conv_second, codebook, codes, upstream):
    grad, sums = window(
        latents,
        conv_first,
        conv_second,
        codebook,
        codes.reshape(8, 128),
        upstream.reshape(CELLS, C),
    )
    grad, sums = hand_over(grad, sums)
    return grad.reshape(upstream.shape), sums


def solution(mesh):
    return jax.shard_map(
        on_device,
        mesh=mesh,
        in_specs=(
            P("tm", "height", None, None),
            P(),
            P(),
            P("height", None),
            P("tm", "height", None),
            P("tm", "height", None, None),
        ),
        out_specs=(P("tm", "height", None, None), P(("height", "tm"), None)),
        check_vma=False,
    )
```

```python
import contextlib

import jax
import jax.numpy as jnp
from jax import lax
from jax.experimental import pallas as pl
from jax.experimental.pallas import tpu as pltpu
from jax.sharding import PartitionSpec as P

F32 = jnp.float32
BF16 = jnp.bfloat16
I32 = jnp.int32
MESH = pl.DeviceIdType.MESH
C = 256
NT, NH = 16, 8
OWN = NT * NH
CAP = 16
SLOTS = OWN * CAP
K_OWN = 2048
CELLS = 1024
VMEM_LIMIT = 60 * 1024 * 1024
STEPS = ((2, 0), (2, 1), (1, 0), (1, 1), (3, 0), (3, 1), (0, 1), (0, 0))


def scope(name):
    return contextlib.nullcontext()


def onehot(cond):
    return jnp.where(cond, 1.0, 0.0).astype(BF16)


def norm_act(values):
    scaled = values * lax.rsqrt(jnp.mean(values * values, -1, keepdims=True) + 1e-06)
    return (scaled / (1.0 + jnp.exp(-scaled))).astype(BF16)


def rotate_back(latent, quant, upward):
    lat_norm = jnp.sqrt(jnp.sum(latent * latent, -1, keepdims=True) + 1e-06)
    quant_norm = jnp.sqrt(jnp.sum(quant * quant, -1, keepdims=True) + 1e-06)
    lat_unit = latent / lat_norm
    quant_unit = quant / quant_norm
    cosine = jnp.sum(lat_unit * quant_unit, -1, keepdims=True)
    summed = lat_unit + quant_unit
    turned = upward - summed * (jnp.sum(summed * upward, -1, keepdims=True) / (1.0 + cosine))
    turned = turned + 2.0 * lat_unit * jnp.sum(quant_unit * upward, -1, keepdims=True)
    return quant_norm / lat_norm * turned + 0.5 * (latent - quant)


def masked(low, high):
    tiles = low.reshape(low.shape[0] // 16, 16, 128)
    return (tiles * jnp.broadcast_to(high, (16, 128)).astype(BF16)[None]).reshape(low.shape)


def column(row):
    return jnp.transpose(jnp.broadcast_to(row, (128, 128)))


def window_kernel(
    lat_hbm,
    w1_ref,
    w2_ref,
    book_ref,
    codes_ref,
    up_hbm,
    grad_hbm,
    sums_hbm,
    lat,
    up,
    wv,
    ext,
    cat,
    acc,
    first,
    enc,
    msg,
    slot,
    rcodes,
    cbuf,
    sbuf,
    rbuf,
    place,
    placed,
    tsend,
    trecv,
    crecv,
    spread_in,
    sums,
    sums_out,
    grad_out,
    in_sem,
    w_sem,
    xs_sem,
    xr_sem,
    ts_sem,
    tr_sem,
    cs_sem,
    cr_sem,
    cb_sem,
    rs_sem,
    rr_sem,
    ks_sem,
    kr_sem,
    gs_sem,
    gr_sem,
    out_sem,
    know,
):
    t = lax.axis_index("tm")
    h = lax.axis_index("height")
    h_up, h_down = lax.rem(h + NH - 1, NH), lax.rem(h + 1, NH)

    def at_h(by):
        return lax.rem(h + by, NH)

    barrier = pltpu.get_barrier_semaphore()

    def if_in(by):
        return pl.when(t + by < NT) if by > 0 else pl.when(t + by >= 0)

    for by in (1, -1):

        @if_in(by)
        def _():
            pl.semaphore_signal(barrier, inc=1, device_id=(t + by, h), device_id_type=MESH)

    for i in range(1, NH):
        pl.semaphore_signal(barrier, inc=1, device_id=(t, at_h(i)), device_id_type=MESH)

    def places(by):
        return lax.div(t + NT - by, NT) + lax.div(2 * NT - 1 - t - by, NT)

    def all_entered():
        pl.semaphore_wait(barrier, NH - 1 + places(1))

    lat_in = [pltpu.make_async_copy(lat_hbm.at[f], lat.at[f], in_sem.at[f]) for f in range(2)]
    up_in = pltpu.make_async_copy(up_hbm, up, in_sem.at[2])
    lat_in[1].start()
    lat_in[0].start()

    def weights_start(c, p):
        w_ref = (w1_ref, w2_ref)[c]
        for q in range(3):
            for r in range(3):
                pltpu.make_async_copy(
                    w_ref.at[p, q, r],
                    wv.at[c, p, pl.ds(q * C, C), pl.ds(r * C, C)],
                    w_sem.at[c, p],
                ).start()

    def weights_here(c, p):
        pltpu.make_async_copy(wv.at[c, p], wv.at[c, p], w_sem.at[c, p]).wait()

    def book_copy(g):
        return pltpu.make_async_copy(
            book_ref.at[pl.ds(g * K_OWN, K_OWN)], cbuf.at[g % 8], cb_sem.at[g % 8]
        )

    def x_copy(c, e, d):
        src, dst, to = ((1, 5, h_up), (4, 0, h_down))[d]
        return pltpu.make_async_remote_copy(
            src_ref=ext.at[c, e, src],
            dst_ref=ext.at[c, e, dst],
            send_sem=xs_sem.at[c, e, d],
            recv_sem=xr_sem.at[c, e, d],
            device_id=(t, to),
            device_id_type=MESH,
        )

    def t_copy(c, e, part):
        rows = (pl.ds(1, 1), pl.ds(4, 1), pl.ds(2, 2))[part]
        return pltpu.make_async_remote_copy(
            src_ref=ext.at[c, e + 2, rows],
            dst_ref=ext.at[c, e, rows],
            send_sem=ts_sem.at[c, e, part],
            recv_sem=tr_sem.at[c, e, part],
            device_id=(lax.rem(t + 1, NT), h),
            device_id_type=MESH,
        )

    def gives_x(d):
        return h > 0 if d == 0 else h < NH - 1

    def takes_x(d):
        return h < NH - 1 if d == 0 else h > 0

    def x_start(c, e, d):
        @pl.when(gives_x(d))
        def _():
            x_copy(c, e, d).start()

    def x_arrived(c, e):
        for d in range(2):

            @pl.when(takes_x(d))
            def _():
                x_copy(c, e, d).wait_recv()

    def column_at(i, sign):
        dx, dc = STEPS[i]
        x = lax.rem(lax.div(h, 2) + 4 + sign * dx, 4)
        return x * 2 + lax.rem(lax.rem(h, 2) + dc, 2)

    def code_copy(i):
        to = column_at(i, 1)
        return pltpu.make_async_remote_copy(
            src_ref=msg.at[pl.ds(pl.multiple_of(to * NT, NT), NT)],
            dst_ref=rcodes.at[:, h],
            send_sem=cs_sem.at[i],
            recv_sem=cr_sem.at[i],
            device_id=(t, to),
            device_id_type=MESH,
        )

    def row_copy(i, g):
        to = column_at(i, 1)
        return pltpu.make_async_remote_copy(
            src_ref=sbuf.at[to, pl.ds(g * CAP, CAP)],
            dst_ref=rbuf.at[h, pl.ds(g * CAP, CAP)],
            send_sem=rs_sem.at[i],
            recv_sem=rr_sem.at[i],
            device_id=(t, to),
            device_id_type=MESH,
        )

    def key_copy(dt):
        to = lax.rem(t + dt, NT)
        return pltpu.make_async_remote_copy(
            src_ref=rcodes.at[to],
            dst_ref=crecv.at[:, t],
            send_sem=ks_sem.at[dt],
            recv_sem=kr_sem.at[dt],
            device_id=(to, h),
            device_id_type=MESH,
        )

    def term_copy(i, k):
        def far(n):
            return lax.rem(2 + 3 * n + lax.div(n, 2) * (3 + 2 * lax.rem(n, 2)), 4)

        y = lax.rem(lax.rem(t, 4) + far(lax.rem(k, 4)), 4)
        z = lax.rem(lax.div(t, 4) + far(lax.div(k, 4)), 4)
        to_t, to_h = z * 4 + y, column_at(i, 1)
        return pltpu.make_async_remote_copy(
            src_ref=tsend.at[pl.ds(pl.multiple_of((to_h * NT + to_t) * CAP, CAP), CAP)],
            dst_ref=trecv.at[pl.ds(pl.multiple_of((i * NT + t) * CAP, CAP), CAP)],
            send_sem=gs_sem,
            recv_sem=gr_sem.at[i // 2],
            device_id=(to_t, to_h),
            device_id_type=MESH,
        )

    def widen(c, e):
        for q in range(3):
            for i in range(4):
                x = ext[c, e, i + q]
                ok = None
                if e < 2:
                    ok = t > 0
                if q == 0 and i == 0:
                    ok = (h > 0) if ok is None else jnp.logical_and(ok, h > 0)
                if q == 2 and i == 3:
                    ok = (h < NH - 1) if ok is None else jnp.logical_and(ok, h < NH - 1)
                if ok is not None:
                    x = jnp.where(ok, x, jnp.zeros_like(x))
                cat[e, pl.ds(i * 128, 128), pl.ds(q * C, C)] = x

    def product(f, c, e, p, fresh=False):
        for m in range(2):
            for n in range(3):
                rows, cols = pl.ds(m * 256, 256), pl.ds(n * C, C)
                part = jnp.dot(cat[e, rows], wv[c, p, :, cols], preferred_element_type=F32)
                acc[f, rows, cols] = part if fresh else acc[f, rows, cols] + part

    col = lax.broadcasted_iota(I32, (128, C), 0)

    def finish(f, i, base):
        rows = pl.ds(i * 128, 128)
        left = pltpu.roll(acc[f, rows, pl.ds(0, C)], 1, 0)
        left = jnp.where(col == 0, 0.0, left)
        right = pltpu.roll(acc[f, rows, pl.ds(2 * C, C)], 127, 0)
        right = jnp.where(col == 127, 0.0, right)
        return (base.astype(F32) + ((left + right) + acc[f, rows, pl.ds(C, C)])).astype(BF16)

    def send_frame(c, f):
        for d in range(2):
            x_start(c, 2 + f, d)

        @pl.when(t < NT - 1)
        def _():
            for part in range(3):
                t_copy(c, f, part).start()

    lane_i = lax.broadcasted_iota(I32, (128, 128), 1)

    def make_slots():
        codes = codes_ref[...]
        blk = lax.shift_right_logical(codes, 11)
        off1 = jnp.bitwise_and(codes, K_OWN - 1) + 1
        sub = lax.broadcasted_iota(I32, (OWN, 128), 0)
        ht = jnp.concatenate(
            [onehot(sub == jnp.broadcast_to(blk[j : j + 1, :], (OWN, 128))) for j in range(8)], 1
        )
        upper = onehot(
            lax.broadcasted_iota(I32, (CELLS, CELLS), 0)
            < lax.broadcasted_iota(I32, (CELLS, CELLS), 1)
        )
        before = jnp.dot(ht, upper, preferred_element_type=F32)
        rank_row = jnp.sum(before * ht.astype(F32), axis=0, keepdims=True)
        rank = jnp.concatenate([rank_row[:, j * 128 : (j + 1) * 128] for j in range(8)], 0)
        slot[...] = blk * CAP + rank.astype(I32)
        hi = lax.shift_right_logical(off1, 6).astype(F32)
        lo = jnp.bitwise_and(off1, 63).astype(F32)
        lane16 = jnp.bitwise_and(lane_i, CAP - 1).astype(F32)
        v_hi, v_lo = [], []
        for j in range(8):
            match = column(rank[j : j + 1, :]) == lane16
            v_hi.append(jnp.where(match, column(hi[j : j + 1, :]), 0.0).astype(BF16))
            v_lo.append(jnp.where(match, column(lo[j : j + 1, :]), 0.0).astype(BF16))
        m_hi = jnp.dot(ht, jnp.concatenate(v_hi, 0), preferred_element_type=F32)
        m_lo = jnp.dot(ht, jnp.concatenate(v_lo, 0), preferred_element_type=F32)
        msg[...] = (m_hi * 64.0 + m_lo).astype(I32)

    group8 = lax.broadcasted_iota(I32, (8, 128), 0)
    mine = lax.shift_right_logical(lax.broadcasted_iota(I32, (8, 128), 1), 4) == group8

    def key_row(tile):
        return jnp.sum(jnp.where(mine, tile, 0), axis=0, keepdims=True) - 1

    def pick_rows(want, tiles):
        want = want.astype(I32)
        low = onehot(jnp.bitwise_and(want, 127) == lane_i)
        high = lax.shift_right_arithmetic(want, 7).astype(F32).astype(BF16)
        return jnp.concatenate(
            [jnp.where(high == float(j), low, jnp.zeros_like(low)) for j in range(tiles)], 1
        )

    def gather(k):
        group = range(4 * k, 4 * k + 4)
        for g in group:
            book_copy(g).wait()
        picks = [
            pick_rows(column(key_row(rcodes[g]).astype(F32)), K_OWN // 128) for g in group
        ]
        for g, pick in zip(group, picks):
            found = jnp.dot(pick, cbuf[g % 8], preferred_element_type=F32).astype(BF16)
            for s in range(NH):
                sbuf[s, pl.ds(g * CAP, CAP)] = found[s * CAP : (s + 1) * CAP]
        for g in group:
            if g + 8 < NT:
                book_copy(g + 8).start()

    def send_rows(*ranges):
        for g in ranges:
            for i in range(NH - 1):
                row_copy(i, g).start()

    def all_rows(i, sem):
        return pltpu.make_async_copy(rbuf.at[i], rbuf.at[i], sem.at[i])

    def tell(r):
        for by in (2**r, -(2**r)):

            @if_in(by)
            def _():
                pl.semaphore_signal(know.at[r], inc=1, device_id=(t + by, h), device_id_type=MESH)

    def told(r):
        pl.semaphore_wait(know.at[r], places(2**r))

    lane = lax.broadcasted_iota(I32, (256, 128), 0)

    def lay_one_hot(ref, lanes_at, row):
        low = onehot(lane == jnp.broadcast_to(jnp.bitwise_and(row, 255), (256, 128)))
        high = lax.shift_right_arithmetic(row, 8)
        for b in range(8):
            ref[pl.ds(b * 256, 256), lanes_at] = masked(low, jnp.where(high == b, 1.0, 0.0))

    def make_place():
        for j in range(8):
            lay_one_hot(place, pl.ds(j * 128, 128), slot[pl.ds(j, 1), :])

    def make_spread():
        for dt in range(1, NT):
            key_copy(dt).wait_recv()
        own_keys.wait()
        for i in range(NH):
            keys = crecv[column_at(i, -1)]
            for half in range(2):
                row = key_row(keys[half * 8 : half * 8 + 8])
                lay_one_hot(spread_in, pl.ds(i * 256 + half * 128, 128), row)

    def next_frame(f):
        with scope("next"):
            for i in range(4):
                x = finish(f, i, lat[f, i])
                first[f, i] = x
                ext[1, 2 + f, 1 + i] = norm_act(x.astype(F32))
        send_frame(1, f)

    def rows_of(c, e):
        with scope("wait_x"):
            x_arrived(c, e)
        with scope("widen"):
            widen(c, e)

    def forward(c, e):
        with scope(f"wait_edge{c}{e}"):

            @pl.when(t > 0)
            def _():
                for d in range(2):
                    t_copy(c, e, d).wait_recv()
                    x_start(c, e, d)

    def earlier_frame(c, e):
        @pl.when(t > 0)
        def _():
            with scope(f"wait_mid{c}{e}"):
                t_copy(c, e, 2).wait_recv()
            with scope(f"wait_fwd{c}{e}"):
                x_arrived(c, e)

    def mm(*args, **kw):
        with scope("mm"):
            product(*args, **kw)

    def fetch(k):
        with scope("gather"):
            gather(k)

    with scope("slots"):
        make_slots()
    for f in (1, 0):
        with scope("latin"):
            lat_in[f].wait()
        with scope("act"):
            for i in range(4):
                ext[0, 2 + f, 1 + i] = norm_act(lat[f, i].astype(F32))
        if f == 1:
            weights_start(0, 2)
            with scope("barrier"):
                all_entered()
        send_frame(0, f)
        if f == 1:
            for i in range(NH - 1):
                code_copy(i).start()
    tell(0)
    for g in range(4):
        book_copy(g).start()
    weights_start(0, 1)
    weights_start(0, 0)
    rcodes[:, h] = msg[pl.ds(pl.multiple_of(h * NT, NT), NT)]
    for g in range(4, 8):
        book_copy(g).start()
    with scope("place"):
        make_place()
    with scope("asked"):
        for i in range(NH - 1):
            code_copy(i).wait_recv()
    fetch(0)
    send_rows(0, 1)
    rows_of(0, 3)
    weights_here(0, 2)
    mm(1, 0, 3, 2, fresh=True)
    rows_of(0, 2)
    forward(0, 1)
    send_rows(2)
    weights_here(0, 1)
    mm(1, 0, 2, 1)
    send_rows(3)
    mm(0, 0, 2, 2, fresh=True)
    for p in (2, 1, 0):
        weights_start(1, p)
    earlier_frame(0, 1)
    weights_here(0, 0)
    with scope("widen"):
        widen(0, 1)
    mm(1, 0, 1, 0)
    next_frame(1)
    fetch(1)
    forward(0, 0)
    send_rows(4)
    mm(0, 0, 1, 1)
    send_rows(5)
    with scope("know"):
        told(0)
    tell(1)
    fetch(2)
    send_rows(6)
    earlier_frame(0, 0)
    send_rows(7)
    with scope("widen"):
        widen(0, 0)
    mm(0, 0, 0, 0)
    next_frame(0)
    send_rows(8)
    with scope("know"):
        told(1)
    tell(2)
    rows_of(1, 3)
    weights_here(1, 2)
    mm(1, 1, 3, 2, fresh=True)
    forward(1, 1)
    send_rows(9)
    fetch(3)
    rbuf[h] = sbuf[h]
    up_in.start()
    send_rows(10)
    with scope("know"):
        told(2)
    tell(3)
    rows_of(1, 2)
    send_rows(11)
    weights_here(1, 1)
    mm(1, 1, 2, 1)
    send_rows(12)
    mm(0, 1, 2, 2, fresh=True)
    earlier_frame(1, 1)
    send_rows(13)
    weights_here(1, 0)
    with scope("widen"):
        widen(1, 1)
    mm(1, 1, 1, 0)
    send_rows(14)
    for i in range(4):
        enc[pl.ds(512 + i * 128, 128)] = finish(1, i, first[1, i])
    mm(0, 1, 1, 1)
    forward(1, 0)
    send_rows(15)
    with scope("know"):
        told(3)
    for i in range(1, NH):
        pl.semaphore_signal(know.at[4], inc=1, device_id=(t, at_h(i)), device_id_type=MESH)
    for dt in range(1, NT):
        key_copy(dt).start()
    own_keys = pltpu.make_async_copy(rcodes.at[t], crecv.at[:, t], kr_sem.at[0])
    own_keys.start()
    with scope("placed"):
        for b in range(4):
            rows = pl.ds(b * 512, 512)
            placed[rows] = jnp.dot(place[rows, 512:], enc[512:], preferred_element_type=F32)
    earlier_frame(1, 0)
    with scope("widen"):
        widen(1, 0)
    mm(0, 1, 0, 0)
    for i in range(4):
        enc[pl.ds(i * 128, 128)] = finish(0, i, first[0, i])
    with scope("know"):
        pl.semaphore_wait(know.at[4], NH - 1)

    with scope("wait_rows"):
        for i in range(NH - 1):
            all_rows(i, rr_sem).wait()

    for chip in range(4):
        to_x = lax.rem(lax.div(h, 2) + STEPS[2 * chip][0], 4)
        rows = pl.ds(pl.multiple_of(to_x * 512, 512), 512)
        with scope("terms"):
            total = placed[rows] + jnp.dot(
                place[rows, :512], enc[:512], preferred_element_type=F32
            )
            pair = rbuf[pl.ds(to_x * 2, 2)].reshape(512, C)
            tsend[rows] = (pair.astype(F32) - total).astype(BF16)

        @pl.loop(0, NT)
        def _(k):
            term_copy(2 * chip, k).start()
            if chip < 3:
                term_copy(2 * chip + 1, k).start()
            else:

                @pl.when(k < NT - 1)
                def _():
                    term_copy(NH - 1, k).start()

    pltpu.make_async_copy(
        tsend.at[pl.ds(pl.multiple_of((h * NT + t) * CAP, CAP), CAP)],
        trecv.at[pl.ds(pl.multiple_of(((NH - 1) * NT + t) * CAP, CAP), CAP)],
        gr_sem.at[3],
    ).start()

    with scope("spread"):
        make_spread()

    with scope("grad"):
        up_in.wait()
        rows_all = rbuf[...].reshape(SLOTS, C)
        for j in range(8):
            pick = pick_rows(column(slot[pl.ds(j, 1), :].astype(F32)), SLOTS // 128)
            quant = jnp.dot(pick, rows_all, preferred_element_type=F32)
            cells = pl.ds(j * 128, 128)
            grad_out[cells] = rotate_back(
                enc[cells].astype(F32), quant, up[cells].astype(F32)
            ).astype(BF16)
    grad_done = pltpu.make_async_copy(grad_out, grad_hbm, out_sem.at[0])
    grad_done.start()

    for i in range(NH - 1):
        code_copy(i).wait_send()
        all_rows(i, rs_sem).wait()
    for dt in range(1, NT):
        key_copy(dt).wait_send()
    for c in range(2):
        for e in range(4):
            for d in range(2):
                given = gives_x(d) if e > 1 else jnp.logical_and(t > 0, gives_x(d))

                @pl.when(given)
                def _():
                    x_copy(c, e, d).wait_send()

        @pl.when(t < NT - 1)
        def _():
            for e in range(2):
                for part in range(3):
                    t_copy(c, e, part).wait_send()

    def arrived(chip):
        part = pl.ds(chip * 512, 512)
        with scope(f"wait_terms{chip}"):
            pltpu.make_async_copy(trecv.at[part], trecv.at[part], gr_sem.at[chip]).wait()

    def summed(rows, part):
        return jnp.dot(spread_in[rows, part], trecv[part], preferred_element_type=F32)

    arrived(0)
    with scope("sums"):
        for b in range(4):
            rows = pl.ds(b * 512, 512)
            sums[rows] = summed(rows, pl.ds(0, 512))
    sent = pl.ds(0, SLOTS - CAP)
    with scope("sent"):
        pltpu.make_async_copy(tsend.at[sent], tsend.at[sent], gs_sem).wait()
    for chip in range(1, 4):
        arrived(chip)
    done = []
    with scope("sums"):
        for b in range(2):
            rows = pl.ds(b * 1024, 1024)
            total = sums[rows] + summed(rows, pl.ds(512, 1536))
            sums_out[rows] = (2.0 * total).astype(BF16)
            copy = pltpu.make_async_copy(sums_out.at[rows], sums_hbm.at[rows], out_sem.at[1 + b])
            copy.start()
            done.append(copy)
    with scope("out"):
        grad_done.wait()
        for copy in done:
            copy.wait()


def window(latents, w1, w2, book, codes, upstream):
    vm = pl.BlockSpec(memory_space=pltpu.VMEM)
    hbm = pl.BlockSpec(memory_space=pl.ANY)
    dma = pltpu.SemaphoreType.DMA
    return pl.pallas_call(
        window_kernel,
        out_shape=(
            jax.ShapeDtypeStruct((CELLS, C), BF16),
            jax.ShapeDtypeStruct((K_OWN, C), BF16),
        ),
        in_specs=[hbm, hbm, hbm, hbm, vm, hbm],
        out_specs=(hbm, hbm),
        scratch_shapes=[
            pltpu.VMEM((2, 4, 128, C), BF16),
            pltpu.VMEM((CELLS, C), BF16),
            pltpu.VMEM((2, 3, 3 * C, 3 * C), BF16),
            pltpu.VMEM((2, 4, 6, 128, C), BF16),
            pltpu.VMEM((4, 512, 3 * C), BF16),
            pltpu.VMEM((2, 512, 3 * C), F32),
            pltpu.VMEM((2, 4, 128, C), BF16),
            pltpu.VMEM((CELLS, C), BF16),
            pltpu.VMEM((OWN, 128), I32),
            pltpu.VMEM((8, 128), I32),
            pltpu.VMEM((NT, NH, 128), I32),
            pltpu.VMEM((8, K_OWN, C), BF16),
            pltpu.VMEM((NH, 256, C), BF16),
            pltpu.VMEM((NH, 256, C), BF16),
            pltpu.VMEM((SLOTS, CELLS), BF16),
            pltpu.VMEM((SLOTS, C), F32),
            pltpu.VMEM((SLOTS, C), BF16),
            pltpu.VMEM((SLOTS, C), BF16),
            pltpu.VMEM((NH, NT, 128), I32),
            pltpu.VMEM((K_OWN, SLOTS), BF16),
            pltpu.VMEM((K_OWN, C), F32),
            pltpu.VMEM((K_OWN, C), BF16),
            pltpu.VMEM((CELLS, C), BF16),
            dma((3,)),
            dma((2, 3)),
            dma((2, 4, 2)),
            dma((2, 4, 2)),
            dma((2, 2, 3)),
            dma((2, 2, 3)),
            dma((NH,)),
            dma((NH,)),
            dma((8,)),
            dma((NH,)),
            dma((NH,)),
            dma((NT,)),
            dma((NT,)),
            dma,
            dma((4,)),
            dma((3,)),
            pltpu.SemaphoreType.REGULAR((5,)),
        ],
        compiler_params=pltpu.CompilerParams(
            collective_id=0, has_side_effects=True, vmem_limit_bytes=VMEM_LIMIT
        ),
        name="window",
    )(latents, w1, w2, book, codes, upstream)


def hand_kernel(grad_in, sums_in, grad_ref, sums_ref, grad_buf, sums_buf, in_sem, out_sem):
    pieces = [(grad_in, grad_buf, grad_ref, 0), (grad_in, grad_buf, grad_ref, 1)] + [
        (sums_in, sums_buf, sums_ref, k) for k in range(4)
    ]
    ins, outs = [], []
    for n, (src, buf, dst, k) in enumerate(pieces):
        rows = pl.ds(k * 512, 512)
        ins.append(pltpu.make_async_copy(src.at[rows], buf.at[rows], in_sem.at[n]))
        outs.append(pltpu.make_async_copy(buf.at[rows], dst.at[rows], out_sem.at[n]))
        ins[-1].start()
    for n in range(len(pieces)):
        ins[n].wait()
        outs[n].start()
    for n in range(len(pieces)):
        outs[n].wait()


def hand_over(grad, sums):
    hbm = pl.BlockSpec(memory_space=pl.ANY)
    dma = pltpu.SemaphoreType.DMA
    return pl.pallas_call(
        hand_kernel,
        out_shape=(
            jax.ShapeDtypeStruct((CELLS, C), BF16),
            jax.ShapeDtypeStruct((K_OWN, C), BF16),
        ),
        in_specs=[hbm, hbm],
        out_specs=(hbm, hbm),
        scratch_shapes=[
            pltpu.VMEM((CELLS, C), BF16),
            pltpu.VMEM((K_OWN, C), BF16),
            dma((6,)),
            dma((6,)),
        ],
        name="hand_over",
    )(grad, sums)


def on_device(latents, conv_first, conv_second, codebook, codes, upstream):
    grad, sums = window(
        latents,
        conv_first,
        conv_second,
        codebook,
        codes.reshape(8, 128),
        upstream.reshape(CELLS, C),
    )
    grad, sums = hand_over(grad, sums)
    return grad.reshape(upstream.shape), sums


def solution(mesh):
    return jax.shard_map(
        on_device,
        mesh=mesh,
        in_specs=(
            P("tm", "height", None, None),
            P(),
            P(),
            P("height", None),
            P("tm", "height", None),
            P("tm", "height", None, None),
        ),
        out_specs=(P("tm", "height", None, None), P(("height", "tm"), None)),
        check_vma=False,
    )
```

```python
import contextlib

import jax
import jax.numpy as jnp
from jax import lax
from jax.experimental import pallas as pl
from jax.experimental.pallas import tpu as pltpu
from jax.sharding import PartitionSpec as P

F32 = jnp.float32
BF16 = jnp.bfloat16
I32 = jnp.int32
MESH = pl.DeviceIdType.MESH
C = 256
NT, NH = 16, 8
OWN = NT * NH
CAP = 16
SLOTS = OWN * CAP
K_OWN = 2048
CELLS = 1024
VMEM_LIMIT = 60 * 1024 * 1024
STEPS = ((2, 0), (2, 1), (1, 0), (1, 1), (3, 0), (3, 1), (0, 1), (0, 0))


def scope(name):
    return contextlib.nullcontext()


def onehot(cond):
    return jnp.where(cond, 1.0, 0.0).astype(BF16)


def norm_act(values):
    scaled = values * lax.rsqrt(jnp.mean(values * values, -1, keepdims=True) + 1e-06)
    return (scaled / (1.0 + jnp.exp(-scaled))).astype(BF16)


def rotate_back(latent, quant, upward):
    lat_norm = jnp.sqrt(jnp.sum(latent * latent, -1, keepdims=True) + 1e-06)
    quant_norm = jnp.sqrt(jnp.sum(quant * quant, -1, keepdims=True) + 1e-06)
    lat_unit = latent / lat_norm
    quant_unit = quant / quant_norm
    cosine = jnp.sum(lat_unit * quant_unit, -1, keepdims=True)
    summed = lat_unit + quant_unit
    turned = upward - summed * (jnp.sum(summed * upward, -1, keepdims=True) / (1.0 + cosine))
    turned = turned + 2.0 * lat_unit * jnp.sum(quant_unit * upward, -1, keepdims=True)
    return quant_norm / lat_norm * turned + 0.5 * (latent - quant)


def masked(low, high):
    tiles = low.reshape(low.shape[0] // 16, 16, 128)
    return (tiles * jnp.broadcast_to(high, (16, 128)).astype(BF16)[None]).reshape(low.shape)


def column(row):
    return jnp.transpose(jnp.broadcast_to(row, (128, 128)))


def window_kernel(
    lat_hbm,
    w1_ref,
    w2_ref,
    book_ref,
    codes_hbm,
    up_hbm,
    grad_hbm,
    sums_hbm,
    lat,
    up,
    codes_ref,
    wv,
    ext,
    cat,
    acc,
    first,
    enc,
    msg,
    slot,
    rcodes,
    cbuf,
    sbuf,
    rbuf,
    place,
    placed,
    tsend,
    trecv,
    crecv,
    spread_in,
    sums,
    sums_out,
    grad_out,
    in_sem,
    w_sem,
    xs_sem,
    xr_sem,
    ts_sem,
    tr_sem,
    cs_sem,
    cr_sem,
    cb_sem,
    rs_sem,
    rr_sem,
    ks_sem,
    kr_sem,
    gs_sem,
    gr_sem,
    out_sem,
    know,
):
    t = lax.axis_index("tm")
    h = lax.axis_index("height")
    h_up, h_down = lax.rem(h + NH - 1, NH), lax.rem(h + 1, NH)

    def at_h(by):
        return lax.rem(h + by, NH)

    lat_in = [pltpu.make_async_copy(lat_hbm.at[f], lat.at[f], in_sem.at[f]) for f in range(2)]
    up_in = pltpu.make_async_copy(up_hbm, up, in_sem.at[2])
    codes_in = pltpu.make_async_copy(codes_hbm, codes_ref, in_sem.at[3])
    lat_in[1].start()
    codes_in.start()
    lat_in[0].start()

    barrier = pltpu.get_barrier_semaphore()

    def if_in(by):
        return pl.when(t + by < NT) if by > 0 else pl.when(t + by >= 0)

    for by in (1, -1):

        @if_in(by)
        def _():
            pl.semaphore_signal(barrier, inc=1, device_id=(t + by, h), device_id_type=MESH)

    for i in range(1, NH):
        pl.semaphore_signal(barrier, inc=1, device_id=(t, at_h(i)), device_id_type=MESH)

    def places(by):
        return lax.div(t + NT - by, NT) + lax.div(2 * NT - 1 - t - by, NT)

    def all_entered():
        pl.semaphore_wait(barrier, NH - 1 + places(1))

    def weights_start(c, p):
        w_ref = (w1_ref, w2_ref)[c]
        for q in range(3):
            for r in range(3):
                pltpu.make_async_copy(
                    w_ref.at[p, q, r],
                    wv.at[c, p, pl.ds(q * C, C), pl.ds(r * C, C)],
                    w_sem.at[c, p],
                ).start()

    def weights_here(c, p):
        pltpu.make_async_copy(wv.at[c, p], wv.at[c, p], w_sem.at[c, p]).wait()

    def book_copy(g):
        return pltpu.make_async_copy(
            book_ref.at[pl.ds(g * K_OWN, K_OWN)], cbuf.at[g % 8], cb_sem.at[g % 8]
        )

    def x_copy(c, e, d):
        src, dst, to = ((1, 5, h_up), (4, 0, h_down))[d]
        return pltpu.make_async_remote_copy(
            src_ref=ext.at[c, e, src],
            dst_ref=ext.at[c, e, dst],
            send_sem=xs_sem.at[d if e > 1 else 2 + d],
            recv_sem=xr_sem.at[c, e, d],
            device_id=(t, to),
            device_id_type=MESH,
        )

    def t_copy(c, e, part):
        rows = (pl.ds(1, 1), pl.ds(4, 1), pl.ds(2, 2))[part]
        return pltpu.make_async_remote_copy(
            src_ref=ext.at[c, e + 2, rows],
            dst_ref=ext.at[c, e, rows],
            send_sem=ts_sem,
            recv_sem=tr_sem.at[c, e, part],
            device_id=(lax.rem(t + 1, NT), h),
            device_id_type=MESH,
        )

    def gives_x(d):
        return h > 0 if d == 0 else h < NH - 1

    def takes_x(d):
        return h < NH - 1 if d == 0 else h > 0

    def x_start(c, e, d):
        @pl.when(gives_x(d))
        def _():
            x_copy(c, e, d).start()

    def x_arrived(c, e):
        for d in range(2):

            @pl.when(takes_x(d))
            def _():
                x_copy(c, e, d).wait_recv()

    def column_at(i, sign):
        dx, dc = STEPS[i]
        x = lax.rem(lax.div(h, 2) + 4 + sign * dx, 4)
        return x * 2 + lax.rem(lax.rem(h, 2) + dc, 2)

    def code_copy(i):
        to = column_at(i, 1)
        return pltpu.make_async_remote_copy(
            src_ref=msg.at[pl.ds(pl.multiple_of(to * NT, NT), NT)],
            dst_ref=rcodes.at[:, h],
            send_sem=cs_sem,
            recv_sem=cr_sem,
            device_id=(t, to),
            device_id_type=MESH,
        )

    def row_copy(i, g):
        to = column_at(i, 1)
        return pltpu.make_async_remote_copy(
            src_ref=sbuf.at[to, pl.ds(g * CAP, CAP)],
            dst_ref=rbuf.at[h, pl.ds(g * CAP, CAP)],
            send_sem=rs_sem,
            recv_sem=rr_sem,
            device_id=(t, to),
            device_id_type=MESH,
        )

    def key_copy(dt):
        to = lax.rem(t + dt, NT)
        return pltpu.make_async_remote_copy(
            src_ref=rcodes.at[to],
            dst_ref=crecv.at[:, t],
            send_sem=ks_sem,
            recv_sem=kr_sem,
            device_id=(to, h),
            device_id_type=MESH,
        )

    def term_copy(i, k):
        def far(n):
            return lax.rem(2 + 3 * n + lax.div(n, 2) * (3 + 2 * lax.rem(n, 2)), 4)

        y = lax.rem(lax.rem(t, 4) + far(lax.rem(k, 4)), 4)
        z = lax.rem(lax.div(t, 4) + far(lax.div(k, 4)), 4)
        to_t, to_h = z * 4 + y, column_at(i, 1)
        return pltpu.make_async_remote_copy(
            src_ref=tsend.at[pl.ds(pl.multiple_of((to_h * NT + to_t) * CAP, CAP), CAP)],
            dst_ref=trecv.at[pl.ds(pl.multiple_of((i * NT + t) * CAP, CAP), CAP)],
            send_sem=gs_sem,
            recv_sem=gr_sem.at[i // 2],
            device_id=(to_t, to_h),
            device_id_type=MESH,
        )

    def widen(c, e):
        for q in range(3):
            for i in range(4):
                x = ext[c, e, i + q]
                ok = None
                if e < 2:
                    ok = t > 0
                if q == 0 and i == 0:
                    ok = (h > 0) if ok is None else jnp.logical_and(ok, h > 0)
                if q == 2 and i == 3:
                    ok = (h < NH - 1) if ok is None else jnp.logical_and(ok, h < NH - 1)
                if ok is not None:
                    x = jnp.where(ok, x, jnp.zeros_like(x))
                cat[e, pl.ds(i * 128, 128), pl.ds(q * C, C)] = x

    def product(f, c, e, p, fresh=False):
        for m in range(2):
            for n in range(3):
                rows, cols = pl.ds(m * 256, 256), pl.ds(n * C, C)
                part = jnp.dot(cat[e, rows], wv[c, p, :, cols], preferred_element_type=F32)
                acc[f, rows, cols] = part if fresh else acc[f, rows, cols] + part

    col = lax.broadcasted_iota(I32, (128, C), 0)

    def finish(f, i, base):
        rows = pl.ds(i * 128, 128)
        left = pltpu.roll(acc[f, rows, pl.ds(0, C)], 1, 0)
        left = jnp.where(col == 0, 0.0, left)
        right = pltpu.roll(acc[f, rows, pl.ds(2 * C, C)], 127, 0)
        right = jnp.where(col == 127, 0.0, right)
        return (base.astype(F32) + ((left + right) + acc[f, rows, pl.ds(C, C)])).astype(BF16)

    def send_frame(c, f):
        for d in range(2):
            x_start(c, 2 + f, d)

        @pl.when(t < NT - 1)
        def _():
            for part in range(3):
                t_copy(c, f, part).start()

    lane_i = lax.broadcasted_iota(I32, (128, 128), 1)

    def make_slots():
        codes = codes_ref[...]
        blk = lax.shift_right_logical(codes, 11)
        off1 = jnp.bitwise_and(codes, K_OWN - 1) + 1
        sub = lax.broadcasted_iota(I32, (OWN, 128), 0)
        ht = jnp.concatenate(
            [onehot(sub == jnp.broadcast_to(blk[j : j + 1, :], (OWN, 128))) for j in range(8)], 1
        )
        upper = onehot(
            lax.broadcasted_iota(I32, (CELLS, CELLS), 0)
            < lax.broadcasted_iota(I32, (CELLS, CELLS), 1)
        )
        before = jnp.dot(ht, upper, preferred_element_type=F32)
        rank_row = jnp.sum(before * ht.astype(F32), axis=0, keepdims=True)
        rank = jnp.concatenate([rank_row[:, j * 128 : (j + 1) * 128] for j in range(8)], 0)
        slot[...] = blk * CAP + rank.astype(I32)
        hi = lax.shift_right_logical(off1, 6).astype(F32)
        lo = jnp.bitwise_and(off1, 63).astype(F32)
        lane16 = jnp.bitwise_and(lane_i, CAP - 1).astype(F32)
        v_hi, v_lo = [], []
        for j in range(8):
            match = column(rank[j : j + 1, :]) == lane16
            v_hi.append(jnp.where(match, column(hi[j : j + 1, :]), 0.0).astype(BF16))
            v_lo.append(jnp.where(match, column(lo[j : j + 1, :]), 0.0).astype(BF16))
        m_hi = jnp.dot(ht, jnp.concatenate(v_hi, 0), preferred_element_type=F32)
        m_lo = jnp.dot(ht, jnp.concatenate(v_lo, 0), preferred_element_type=F32)
        msg[...] = (m_hi * 64.0 + m_lo).astype(I32)

    group8 = lax.broadcasted_iota(I32, (8, 128), 0)
    mine = lax.shift_right_logical(lax.broadcasted_iota(I32, (8, 128), 1), 4) == group8

    def key_row(tile):
        return jnp.sum(jnp.where(mine, tile, 0), axis=0, keepdims=True) - 1

    def pick_rows(want, tiles):
        want = want.astype(I32)
        low = onehot(jnp.bitwise_and(want, 127) == lane_i)
        high = lax.shift_right_arithmetic(want, 7).astype(F32).astype(BF16)
        return jnp.concatenate(
            [jnp.where(high == float(j), low, jnp.zeros_like(low)) for j in range(tiles)], 1
        )

    def gather(k):
        group = range(4 * k, 4 * k + 4)
        for g in group:
            book_copy(g).wait()
        picks = [
            pick_rows(column(key_row(rcodes[g]).astype(F32)), K_OWN // 128) for g in group
        ]
        for g, pick in zip(group, picks):
            found = jnp.dot(pick, cbuf[g % 8], preferred_element_type=F32).astype(BF16)
            for s in range(NH):
                sbuf[s, pl.ds(g * CAP, CAP)] = found[s * CAP : (s + 1) * CAP]
        for g in group:
            if g + 8 < NT:
                book_copy(g + 8).start()

    def send_rows(*ranges):
        for g in ranges:
            for i in range(NH - 1):
                row_copy(i, g).start()

    def bytes_of(ref, sem):
        pltpu.make_async_copy(ref, ref, sem).wait()

    def tell(r):
        for by in (2**r, -(2**r)):

            @if_in(by)
            def _():
                pl.semaphore_signal(know.at[r], inc=1, device_id=(t + by, h), device_id_type=MESH)

    def told(r):
        pl.semaphore_wait(know.at[r], places(2**r))

    lane = lax.broadcasted_iota(I32, (256, 128), 0)

    def lay_one_hot(ref, lanes_at, row):
        low = onehot(lane == jnp.broadcast_to(jnp.bitwise_and(row, 255), (256, 128)))
        high = lax.shift_right_arithmetic(row, 8)
        for b in range(8):
            ref[pl.ds(b * 256, 256), lanes_at] = masked(low, jnp.where(high == b, 1.0, 0.0))

    def make_place():
        for j in range(8):
            lay_one_hot(place, pl.ds(j * 128, 128), slot[pl.ds(j, 1), :])

    def make_spread():
        bytes_of(crecv, kr_sem)
        for i in range(NH):
            keys = crecv[column_at(i, -1)]
            for half in range(2):
                row = key_row(keys[half * 8 : half * 8 + 8])
                lay_one_hot(spread_in, pl.ds(i * 256 + half * 128, 128), row)

    def next_frame(f):
        with scope("next"):
            for i in range(4):
                x = finish(f, i, lat[f, i])
                first[f, i] = x
                ext[1, 2 + f, 1 + i] = norm_act(x.astype(F32))
        send_frame(1, f)

    def rows_of(c, e):
        with scope("wait_x"):
            x_arrived(c, e)
        with scope("widen"):
            widen(c, e)

    def forward(c, e):
        with scope(f"wait_edge{c}{e}"):

            @pl.when(t > 0)
            def _():
                for d in range(2):
                    t_copy(c, e, d).wait_recv()
                    x_start(c, e, d)

    def earlier_frame(c, e):
        @pl.when(t > 0)
        def _():
            with scope(f"wait_mid{c}{e}"):
                t_copy(c, e, 2).wait_recv()
            with scope(f"wait_fwd{c}{e}"):
                x_arrived(c, e)

    def mm(*args, **kw):
        with scope("mm"):
            product(*args, **kw)

    def fetch(k):
        with scope("gather"):
            gather(k)

    for f in (1, 0):
        with scope("latin"):
            lat_in[f].wait()
        with scope("act"):
            for i in range(4):
                ext[0, 2 + f, 1 + i] = norm_act(lat[f, i].astype(F32))
        if f == 1:
            with scope("barrier"):
                all_entered()
        send_frame(0, f)
        if f == 1:
            tell(0)
            with scope("slots"):
                codes_in.wait()
                make_slots()
            for i in range(NH - 1):
                code_copy(i).start()
    weights_start(0, 2)
    for g in range(4):
        book_copy(g).start()
    weights_start(0, 1)
    weights_start(0, 0)
    rcodes[:, h] = msg[pl.ds(pl.multiple_of(h * NT, NT), NT)]
    for g in range(4, 8):
        book_copy(g).start()
    with scope("place"):
        make_place()
    rows_of(0, 3)
    weights_here(0, 2)
    mm(1, 0, 3, 2, fresh=True)
    with scope("asked"):
        bytes_of(msg.at[pl.ds(0, OWN - NT)], cr_sem)
    fetch(0)
    send_rows(0, 1)
    rows_of(0, 2)
    forward(0, 1)
    send_rows(2)
    weights_here(0, 1)
    mm(1, 0, 2, 1)
    send_rows(3)
    mm(0, 0, 2, 2, fresh=True)
    fetch(1)
    send_rows(4)
    with scope("know"):
        told(0)
    tell(1)
    for p in (2, 1, 0):
        weights_start(1, p)
    fetch(2)
    earlier_frame(0, 1)
    forward(0, 0)
    send_rows(5, 6)
    weights_here(0, 0)
    with scope("widen"):
        widen(0, 1)
    mm(1, 0, 1, 0)
    next_frame(1)
    send_rows(7)
    mm(0, 0, 1, 1)
    with scope("know"):
        told(1)
    tell(2)
    send_rows(8)
    fetch(3)
    rbuf[h] = sbuf[h]
    up_in.start()
    earlier_frame(0, 0)
    send_rows(9)
    with scope("widen"):
        widen(0, 0)
    mm(0, 0, 0, 0)
    next_frame(0)
    forward(1, 1)
    send_rows(10)
    with scope("know"):
        told(2)
    tell(3)
    rows_of(1, 3)
    send_rows(11)
    weights_here(1, 2)
    mm(1, 1, 3, 2, fresh=True)
    send_rows(12)
    rows_of(1, 2)
    send_rows(13)
    weights_here(1, 1)
    mm(1, 1, 2, 1)
    send_rows(14)
    mm(0, 1, 2, 2, fresh=True)
    send_rows(15)
    with scope("know"):
        told(3)
    for i in range(1, NH):
        pl.semaphore_signal(know.at[4], inc=1, device_id=(t, at_h(i)), device_id_type=MESH)
    earlier_frame(1, 1)
    forward(1, 0)
    weights_here(1, 0)
    with scope("widen"):
        widen(1, 1)
    mm(1, 1, 1, 0)
    for i in range(4):
        enc[pl.ds(512 + i * 128, 128)] = finish(1, i, first[1, i])
    mm(0, 1, 1, 1)
    for dt in range(1, NT):
        key_copy(dt).start()
    pltpu.make_async_copy(rcodes.at[t], crecv.at[:, t], kr_sem).start()
    with scope("placed"):
        for b in range(4):
            rows = pl.ds(b * 512, 512)
            placed[rows] = jnp.dot(place[rows, 512:], enc[512:], preferred_element_type=F32)
    earlier_frame(1, 0)
    with scope("widen"):
        widen(1, 0)
    mm(0, 1, 0, 0)
    for i in range(4):
        enc[pl.ds(i * 128, 128)] = finish(0, i, first[0, i])
    with scope("know"):
        pl.semaphore_wait(know.at[4], NH - 1)

    with scope("wait_rows"):
        bytes_of(rbuf.at[pl.ds(0, NH - 1)], rr_sem)

    for chip in range(4):
        to_x = lax.rem(lax.div(h, 2) + STEPS[2 * chip][0], 4)
        rows = pl.ds(pl.multiple_of(to_x * 512, 512), 512)
        with scope("terms"):
            total = placed[rows] + jnp.dot(
                place[rows, :512], enc[:512], preferred_element_type=F32
            )
            pair = rbuf[pl.ds(to_x * 2, 2)].reshape(512, C)
            tsend[rows] = (pair.astype(F32) - total).astype(BF16)

        @pl.loop(0, NT)
        def _(k):
            term_copy(2 * chip, k).start()
            if chip < 3:
                term_copy(2 * chip + 1, k).start()
            else:

                @pl.when(k < NT - 1)
                def _():
                    term_copy(NH - 1, k).start()

    pltpu.make_async_copy(
        tsend.at[pl.ds(pl.multiple_of((h * NT + t) * CAP, CAP), CAP)],
        trecv.at[pl.ds(pl.multiple_of(((NH - 1) * NT + t) * CAP, CAP), CAP)],
        gr_sem.at[3],
    ).start()

    with scope("spread"):
        make_spread()

    with scope("grad"):
        up_in.wait()
        rows_all = rbuf[...].reshape(SLOTS, C)
        for j in range(8):
            pick = pick_rows(column(slot[pl.ds(j, 1), :].astype(F32)), SLOTS // 128)
            quant = jnp.dot(pick, rows_all, preferred_element_type=F32)
            cells = pl.ds(j * 128, 128)
            grad_out[cells] = rotate_back(
                enc[cells].astype(F32), quant, up[cells].astype(F32)
            ).astype(BF16)
    grad_done = pltpu.make_async_copy(grad_out, grad_hbm, out_sem.at[0])
    grad_done.start()

    bytes_of(msg.at[pl.ds(0, OWN - NT)], cs_sem)
    bytes_of(rbuf.at[pl.ds(0, NH - 1)], rs_sem)
    bytes_of(rcodes.at[pl.ds(0, NT - 1)], ks_sem)
    for d in range(2):

        @pl.when(gives_x(d))
        def _():
            bytes_of(ext.at[0, 0, pl.ds(0, 4)], xs_sem.at[d])

        @pl.when(jnp.logical_and(t > 0, gives_x(d)))
        def _():
            bytes_of(ext.at[0, 0, pl.ds(0, 4)], xs_sem.at[2 + d])

    @pl.when(t < NT - 1)
    def _():
        bytes_of(rbuf, ts_sem)

    def arrived(chip):
        part = pl.ds(chip * 512, 512)
        with scope(f"wait_terms{chip}"):
            pltpu.make_async_copy(trecv.at[part], trecv.at[part], gr_sem.at[chip]).wait()

    def summed(rows, part):
        return jnp.dot(spread_in[rows, part], trecv[part], preferred_element_type=F32)

    arrived(0)
    with scope("sums"):
        for b in range(4):
            rows = pl.ds(b * 512, 512)
            sums[rows] = summed(rows, pl.ds(0, 512))
    sent = pl.ds(0, SLOTS - CAP)
    with scope("sent"):
        pltpu.make_async_copy(tsend.at[sent], tsend.at[sent], gs_sem).wait()
    arrived(1)
    with scope("sums"):
        for b in range(4):
            rows = pl.ds(b * 512, 512)
            sums[rows] += summed(rows, pl.ds(512, 512))
    arrived(2)
    arrived(3)
    done = []
    with scope("sums"):
        for b in range(2):
            rows = pl.ds(b * 1024, 1024)
            total = sums[rows] + summed(rows, pl.ds(1024, 1024))
            sums_out[rows] = (2.0 * total).astype(BF16)
            for n in range(2):
                rows = pl.ds(b * 1024 + n * 512, 512)
                copy = pltpu.make_async_copy(
                    sums_out.at[rows], sums_hbm.at[rows], out_sem.at[1 + 2 * b + n]
                )
                copy.start()
                done.append(copy)
    with scope("out"):
        grad_done.wait()
        for copy in done:
            copy.wait()


def window(latents, w1, w2, book, codes, upstream):
    hbm = pl.BlockSpec(memory_space=pl.ANY)
    dma = pltpu.SemaphoreType.DMA
    return pl.pallas_call(
        window_kernel,
        out_shape=(
            jax.ShapeDtypeStruct((CELLS, C), BF16),
            jax.ShapeDtypeStruct((K_OWN, C), BF16),
        ),
        in_specs=[hbm] * 6,
        out_specs=(hbm, hbm),
        scratch_shapes=[
            pltpu.VMEM((2, 4, 128, C), BF16),
            pltpu.VMEM((CELLS, C), BF16),
            pltpu.VMEM((8, 128), I32),
            pltpu.VMEM((2, 3, 3 * C, 3 * C), BF16),
            pltpu.VMEM((2, 4, 6, 128, C), BF16),
            pltpu.VMEM((4, 512, 3 * C), BF16),
            pltpu.VMEM((2, 512, 3 * C), F32),
            pltpu.VMEM((2, 4, 128, C), BF16),
            pltpu.VMEM((CELLS, C), BF16),
            pltpu.VMEM((OWN, 128), I32),
            pltpu.VMEM((8, 128), I32),
            pltpu.VMEM((NT, NH, 128), I32),
            pltpu.VMEM((8, K_OWN, C), BF16),
            pltpu.VMEM((NH, 256, C), BF16),
            pltpu.VMEM((NH, 256, C), BF16),
            pltpu.VMEM((SLOTS, CELLS), BF16),
            pltpu.VMEM((SLOTS, C), F32),
            pltpu.VMEM((SLOTS, C), BF16),
            pltpu.VMEM((SLOTS, C), BF16),
            pltpu.VMEM((NH, NT, 128), I32),
            pltpu.VMEM((K_OWN, SLOTS), BF16),
            pltpu.VMEM((K_OWN, C), F32),
            pltpu.VMEM((K_OWN, C), BF16),
            pltpu.VMEM((CELLS, C), BF16),
            dma((4,)),
            dma((2, 3)),
            dma((4,)),
            dma((2, 4, 2)),
            dma,
            dma((2, 2, 3)),
            dma,
            dma,
            dma((8,)),
            dma,
            dma,
            dma,
            dma,
            dma,
            dma((4,)),
            dma((5,)),
            pltpu.SemaphoreType.REGULAR((5,)),
        ],
        compiler_params=pltpu.CompilerParams(
            collective_id=0, has_side_effects=True, vmem_limit_bytes=VMEM_LIMIT
        ),
        name="window",
    )(latents, w1, w2, book, codes, upstream)


def hand_kernel(grad_in, sums_in, grad_ref, sums_ref, grad_buf, sums_buf, in_sem, out_sem):
    pieces = [(grad_in, grad_buf, grad_ref, k) for k in range(2)] + [
        (sums_in, sums_buf, sums_ref, k) for k in range(4)
    ]
    ins, outs = [], []
    for n, (src, buf, dst, k) in enumerate(pieces):
        rows = pl.ds(k * 512, 512)
        ins.append(pltpu.make_async_copy(src.at[rows], buf.at[rows], in_sem.at[n]))
        outs.append(pltpu.make_async_copy(buf.at[rows], dst.at[rows], out_sem.at[n]))
        ins[-1].start()
    for n in range(len(pieces)):
        ins[n].wait()
        outs[n].start()
    for n in range(len(pieces)):
        outs[n].wait()


def hand_over(grad, sums):
    hbm = pl.BlockSpec(memory_space=pl.ANY)
    dma = pltpu.SemaphoreType.DMA
    return pl.pallas_call(
        hand_kernel,
        out_shape=(
            jax.ShapeDtypeStruct((CELLS, C), BF16),
            jax.ShapeDtypeStruct((K_OWN, C), BF16),
        ),
        in_specs=[hbm, hbm],
        out_specs=(hbm, hbm),
        scratch_shapes=[
            pltpu.VMEM((CELLS, C), BF16),
            pltpu.VMEM((K_OWN, C), BF16),
            dma((6,)),
            dma((6,)),
        ],
        name="hand_over",
    )(grad, sums)


def on_device(latents, conv_first, conv_second, codebook, codes, upstream):
    grad, sums = window(
        latents,
        conv_first,
        conv_second,
        codebook,
        codes.reshape(8, 128),
        upstream.reshape(CELLS, C),
    )
    grad, sums = hand_over(grad, sums)
    return grad.reshape(upstream.shape), sums


def solution(mesh):
    return jax.shard_map(
        on_device,
        mesh=mesh,
        in_specs=(
            P("tm", "height", None, None),
            P(),
            P(),
            P("height", None),
            P("tm", "height", None),
            P("tm", "height", None, None),
        ),
        out_specs=(P("tm", "height", None, None), P(("height", "tm"), None)),
        check_vma=False,
    )
```

```python
import contextlib

import jax
import jax.numpy as jnp
from jax import lax
from jax.experimental import pallas as pl
from jax.experimental.pallas import tpu as pltpu
from jax.sharding import PartitionSpec as P

F32 = jnp.float32
BF16 = jnp.bfloat16
I32 = jnp.int32
MESH = pl.DeviceIdType.MESH
C = 256
NT, NH = 16, 8
OWN = NT * NH
CAP = 16
SLOTS = OWN * CAP
K_OWN = 2048
CELLS = 1024
VMEM_LIMIT = 60 * 1024 * 1024
STEPS = ((2, 0), (2, 1), (1, 0), (1, 1), (3, 0), (3, 1), (0, 1), (0, 0))


def scope(name):
    return contextlib.nullcontext()


def onehot(cond):
    return jnp.where(cond, 1.0, 0.0).astype(BF16)


def norm_act(values):
    scaled = values * lax.rsqrt(jnp.mean(values * values, -1, keepdims=True) + 1e-06)
    return (scaled / (1.0 + jnp.exp(-scaled))).astype(BF16)


def rotate_back(latent, quant, upward):
    lat_norm = jnp.sqrt(jnp.sum(latent * latent, -1, keepdims=True) + 1e-06)
    quant_norm = jnp.sqrt(jnp.sum(quant * quant, -1, keepdims=True) + 1e-06)
    lat_unit = latent / lat_norm
    quant_unit = quant / quant_norm
    cosine = jnp.sum(lat_unit * quant_unit, -1, keepdims=True)
    summed = lat_unit + quant_unit
    turned = upward - summed * (jnp.sum(summed * upward, -1, keepdims=True) / (1.0 + cosine))
    turned = turned + 2.0 * lat_unit * jnp.sum(quant_unit * upward, -1, keepdims=True)
    return quant_norm / lat_norm * turned + 0.5 * (latent - quant)


def masked(low, high):
    tiles = low.reshape(low.shape[0] // 16, 16, 128)
    return (tiles * jnp.broadcast_to(high, (16, 128)).astype(BF16)[None]).reshape(low.shape)


def column(row):
    return jnp.transpose(jnp.broadcast_to(row, (128, 128)))


def window_kernel(
    lat_hbm,
    w1_ref,
    w2_ref,
    book_ref,
    codes_hbm,
    up_hbm,
    grad_hbm,
    sums_hbm,
    lat,
    up,
    codes_ref,
    wv,
    ext,
    cat,
    acc,
    first,
    enc,
    msg,
    slot,
    rcodes,
    cbuf,
    sbuf,
    rbuf,
    place,
    placed,
    tsend,
    trecv,
    crecv,
    spread_in,
    sums,
    sums_out,
    grad_out,
    in_sem,
    w_sem,
    xs_sem,
    xr_sem,
    ts_sem,
    tr_sem,
    cs_sem,
    cr_sem,
    cb_sem,
    rs_sem,
    rr_sem,
    ks_sem,
    kr_sem,
    gs_sem,
    gr_sem,
    out_sem,
    know,
):
    t = lax.axis_index("tm")
    h = lax.axis_index("height")
    h_up, h_down = lax.rem(h + NH - 1, NH), lax.rem(h + 1, NH)

    def at_h(by):
        return lax.rem(h + by, NH)

    lat_in = [pltpu.make_async_copy(lat_hbm.at[f], lat.at[f], in_sem.at[f]) for f in range(2)]
    up_in = pltpu.make_async_copy(up_hbm, up, in_sem.at[2])
    codes_in = pltpu.make_async_copy(codes_hbm, codes_ref, in_sem.at[3])
    lat_in[1].start()
    codes_in.start()
    lat_in[0].start()

    barrier = pltpu.get_barrier_semaphore()

    def if_in(by):
        return pl.when(t + by < NT) if by > 0 else pl.when(t + by >= 0)

    for by in (1, -1):

        @if_in(by)
        def _():
            pl.semaphore_signal(barrier, inc=1, device_id=(t + by, h), device_id_type=MESH)

    for i in range(1, NH):
        pl.semaphore_signal(barrier, inc=1, device_id=(t, at_h(i)), device_id_type=MESH)

    def places(by):
        return lax.div(t + NT - by, NT) + lax.div(2 * NT - 1 - t - by, NT)

    def all_entered():
        pl.semaphore_wait(barrier, NH - 1 + places(1))

    def weights_start(c, p):
        w_ref = (w1_ref, w2_ref)[c]
        for q in range(3):
            for r in range(3):
                pltpu.make_async_copy(
                    w_ref.at[p, q, r],
                    wv.at[c, p, pl.ds(q * C, C), pl.ds(r * C, C)],
                    w_sem.at[c, p],
                ).start()

    def weights_here(c, p):
        pltpu.make_async_copy(wv.at[c, p], wv.at[c, p], w_sem.at[c, p]).wait()

    def book_copy(g):
        return pltpu.make_async_copy(
            book_ref.at[pl.ds(g * K_OWN, K_OWN)], cbuf.at[g % 8], cb_sem.at[g % 8]
        )

    def x_copy(c, e, d):
        src, dst, to = ((1, 5, h_up), (4, 0, h_down))[d]
        return pltpu.make_async_remote_copy(
            src_ref=ext.at[c, e, src],
            dst_ref=ext.at[c, e, dst],
            send_sem=xs_sem.at[d if e > 1 else 2 + d],
            recv_sem=xr_sem.at[c, e, d],
            device_id=(t, to),
            device_id_type=MESH,
        )

    def t_copy(c, e, part):
        rows = (pl.ds(1, 1), pl.ds(4, 1), pl.ds(2, 2))[part]
        return pltpu.make_async_remote_copy(
            src_ref=ext.at[c, e + 2, rows],
            dst_ref=ext.at[c, e, rows],
            send_sem=ts_sem,
            recv_sem=tr_sem.at[c, e, part],
            device_id=(lax.rem(t + 1, NT), h),
            device_id_type=MESH,
        )

    def gives_x(d):
        return h > 0 if d == 0 else h < NH - 1

    def takes_x(d):
        return h < NH - 1 if d == 0 else h > 0

    def x_start(c, e, d):
        @pl.when(gives_x(d))
        def _():
            x_copy(c, e, d).start()

    def x_arrived(c, e):
        for d in range(2):

            @pl.when(takes_x(d))
            def _():
                x_copy(c, e, d).wait_recv()

    def column_at(i, sign):
        dx, dc = STEPS[i]
        x = lax.rem(lax.div(h, 2) + 4 + sign * dx, 4)
        return x * 2 + lax.rem(lax.rem(h, 2) + dc, 2)

    def code_copy(i):
        to = column_at(i, 1)
        return pltpu.make_async_remote_copy(
            src_ref=msg.at[pl.ds(pl.multiple_of(to * NT, NT), NT)],
            dst_ref=rcodes.at[:, h],
            send_sem=cs_sem,
            recv_sem=cr_sem,
            device_id=(t, to),
            device_id_type=MESH,
        )

    def row_copy(i, g):
        to = column_at(i, 1)
        return pltpu.make_async_remote_copy(
            src_ref=sbuf.at[to, pl.ds(g * CAP, CAP)],
            dst_ref=rbuf.at[h, pl.ds(g * CAP, CAP)],
            send_sem=rs_sem,
            recv_sem=rr_sem,
            device_id=(t, to),
            device_id_type=MESH,
        )

    def key_copy(dt):
        to = lax.rem(t + dt, NT)
        return pltpu.make_async_remote_copy(
            src_ref=rcodes.at[to],
            dst_ref=crecv.at[:, t],
            send_sem=ks_sem,
            recv_sem=kr_sem,
            device_id=(to, h),
            device_id_type=MESH,
        )

    def term_copy(i, k):
        def far(n):
            return lax.rem(2 + 3 * n + lax.div(n, 2) * (3 + 2 * lax.rem(n, 2)), 4)

        y = lax.rem(lax.rem(t, 4) + far(lax.rem(k, 4)), 4)
        z = lax.rem(lax.div(t, 4) + far(lax.div(k, 4)), 4)
        to_t, to_h = z * 4 + y, column_at(i, 1)
        return pltpu.make_async_remote_copy(
            src_ref=tsend.at[pl.ds(pl.multiple_of((to_h * NT + to_t) * CAP, CAP), CAP)],
            dst_ref=trecv.at[pl.ds(pl.multiple_of((i * NT + t) * CAP, CAP), CAP)],
            send_sem=gs_sem,
            recv_sem=gr_sem.at[i // 2],
            device_id=(to_t, to_h),
            device_id_type=MESH,
        )

    def widen(c, e):
        for q in range(3):
            for i in range(4):
                x = ext[c, e, i + q]
                ok = None
                if e < 2:
                    ok = t > 0
                if q == 0 and i == 0:
                    ok = (h > 0) if ok is None else jnp.logical_and(ok, h > 0)
                if q == 2 and i == 3:
                    ok = (h < NH - 1) if ok is None else jnp.logical_and(ok, h < NH - 1)
                if ok is not None:
                    x = jnp.where(ok, x, jnp.zeros_like(x))
                cat[e, pl.ds(i * 128, 128), pl.ds(q * C, C)] = x

    def product(f, c, e, p, fresh=False):
        for m in range(2):
            for n in range(3):
                rows, cols = pl.ds(m * 256, 256), pl.ds(n * C, C)
                part = jnp.dot(cat[e, rows], wv[c, p, :, cols], preferred_element_type=F32)
                acc[f, rows, cols] = part if fresh else acc[f, rows, cols] + part

    col = lax.broadcasted_iota(I32, (128, C), 0)

    def finish(f, i, base):
        rows = pl.ds(i * 128, 128)
        left = pltpu.roll(acc[f, rows, pl.ds(0, C)], 1, 0)
        left = jnp.where(col == 0, 0.0, left)
        right = pltpu.roll(acc[f, rows, pl.ds(2 * C, C)], 127, 0)
        right = jnp.where(col == 127, 0.0, right)
        return (base.astype(F32) + ((left + right) + acc[f, rows, pl.ds(C, C)])).astype(BF16)

    def send_frame(c, f):
        for d in range(2):
            x_start(c, 2 + f, d)

        @pl.when(t < NT - 1)
        def _():
            for part in range(3):
                t_copy(c, f, part).start()

    lane_i = lax.broadcasted_iota(I32, (128, 128), 1)

    def make_slots():
        codes = codes_ref[...]
        blk = lax.shift_right_logical(codes, 11)
        off1 = jnp.bitwise_and(codes, K_OWN - 1) + 1
        sub = lax.broadcasted_iota(I32, (OWN, 128), 0)
        ht = jnp.concatenate(
            [onehot(sub == jnp.broadcast_to(blk[j : j + 1, :], (OWN, 128))) for j in range(8)], 1
        )
        upper = onehot(
            lax.broadcasted_iota(I32, (CELLS, CELLS), 0)
            < lax.broadcasted_iota(I32, (CELLS, CELLS), 1)
        )
        before = jnp.dot(ht, upper, preferred_element_type=F32)
        rank_row = jnp.sum(before * ht.astype(F32), axis=0, keepdims=True)
        rank = jnp.concatenate([rank_row[:, j * 128 : (j + 1) * 128] for j in range(8)], 0)
        slot[...] = blk * CAP + rank.astype(I32)
        hi = lax.shift_right_logical(off1, 6).astype(F32)
        lo = jnp.bitwise_and(off1, 63).astype(F32)
        lane16 = jnp.bitwise_and(lane_i, CAP - 1).astype(F32)
        v_hi, v_lo = [], []
        for j in range(8):
            match = column(rank[j : j + 1, :]) == lane16
            v_hi.append(jnp.where(match, column(hi[j : j + 1, :]), 0.0).astype(BF16))
            v_lo.append(jnp.where(match, column(lo[j : j + 1, :]), 0.0).astype(BF16))
        m_hi = jnp.dot(ht, jnp.concatenate(v_hi, 0), preferred_element_type=F32)
        m_lo = jnp.dot(ht, jnp.concatenate(v_lo, 0), preferred_element_type=F32)
        msg[...] = (m_hi * 64.0 + m_lo).astype(I32)

    group8 = lax.broadcasted_iota(I32, (8, 128), 0)
    mine = lax.shift_right_logical(lax.broadcasted_iota(I32, (8, 128), 1), 4) == group8

    def key_row(tile):
        return jnp.sum(jnp.where(mine, tile, 0), axis=0, keepdims=True) - 1

    def pick_rows(want, tiles):
        want = want.astype(I32)
        low = onehot(jnp.bitwise_and(want, 127) == lane_i)
        high = lax.shift_right_arithmetic(want, 7).astype(F32).astype(BF16)
        return jnp.concatenate(
            [jnp.where(high == float(j), low, jnp.zeros_like(low)) for j in range(tiles)], 1
        )

    def gather(k):
        group = range(4 * k, 4 * k + 4)
        for g in group:
            book_copy(g).wait()
        picks = [
            pick_rows(column(key_row(rcodes[g]).astype(F32)), K_OWN // 128) for g in group
        ]
        for g, pick in zip(group, picks):
            found = jnp.dot(pick, cbuf[g % 8], preferred_element_type=F32).astype(BF16)
            for s in range(NH):
                sbuf[s, pl.ds(g * CAP, CAP)] = found[s * CAP : (s + 1) * CAP]
        for g in group:
            if g + 8 < NT:
                book_copy(g + 8).start()

    def send_rows(*ranges):
        for g in ranges:
            for i in range(NH - 1):
                row_copy(i, g).start()

    def bytes_of(ref, sem):
        pltpu.make_async_copy(ref, ref, sem).wait()

    def tell(r):
        for by in (2**r, -(2**r)):

            @if_in(by)
            def _():
                pl.semaphore_signal(know.at[r], inc=1, device_id=(t + by, h), device_id_type=MESH)

    def told(r):
        pl.semaphore_wait(know.at[r], places(2**r))

    lane = lax.broadcasted_iota(I32, (256, 128), 0)

    def lay_one_hot(ref, lanes_at, row):
        low = onehot(lane == jnp.broadcast_to(jnp.bitwise_and(row, 255), (256, 128)))
        high = lax.shift_right_arithmetic(row, 8)
        for b in range(8):
            ref[pl.ds(b * 256, 256), lanes_at] = masked(low, jnp.where(high == b, 1.0, 0.0))

    def make_place():
        for j in range(8):
            lay_one_hot(place, pl.ds(j * 128, 128), slot[pl.ds(j, 1), :])

    def make_spread():
        bytes_of(crecv, kr_sem)
        for i in range(NH):
            keys = crecv[column_at(i, -1)]
            for half in range(2):
                row = key_row(keys[half * 8 : half * 8 + 8])
                lay_one_hot(spread_in, pl.ds(i * 256 + half * 128, 128), row)

    def next_frame(f):
        with scope("next"):
            for i in range(4):
                x = finish(f, i, lat[f, i])
                first[f, i] = x
                ext[1, 2 + f, 1 + i] = norm_act(x.astype(F32))
        send_frame(1, f)

    def rows_of(c, e):
        with scope("wait_x"):
            x_arrived(c, e)
        with scope("widen"):
            widen(c, e)

    def forward(c, e):
        with scope(f"wait_edge{c}{e}"):

            @pl.when(t > 0)
            def _():
                for d in range(2):
                    t_copy(c, e, d).wait_recv()
                    x_start(c, e, d)

    def earlier_frame(c, e):
        @pl.when(t > 0)
        def _():
            with scope(f"wait_mid{c}{e}"):
                t_copy(c, e, 2).wait_recv()
            with scope(f"wait_fwd{c}{e}"):
                x_arrived(c, e)

    def mm(*args, **kw):
        with scope("mm"):
            product(*args, **kw)

    def fetch(k):
        with scope("gather"):
            gather(k)

    for f in (1, 0):
        with scope("latin"):
            lat_in[f].wait()
        with scope("act"):
            for i in range(4):
                ext[0, 2 + f, 1 + i] = norm_act(lat[f, i].astype(F32))
        if f == 1:
            with scope("barrier"):
                all_entered()
        send_frame(0, f)
        if f == 1:
            tell(0)
            with scope("slots"):
                codes_in.wait()
                make_slots()
            for i in range(NH - 1):
                code_copy(i).start()
    weights_start(0, 2)
    for g in range(4):
        book_copy(g).start()
    weights_start(0, 1)
    weights_start(0, 0)
    rcodes[:, h] = msg[pl.ds(pl.multiple_of(h * NT, NT), NT)]
    for g in range(4, 8):
        book_copy(g).start()
    with scope("place"):
        make_place()
    rows_of(0, 3)
    weights_here(0, 2)
    mm(1, 0, 3, 2, fresh=True)
    with scope("asked"):
        bytes_of(msg.at[pl.ds(0, OWN - NT)], cr_sem)
    fetch(0)
    send_rows(0, 1)
    rows_of(0, 2)
    forward(0, 1)
    send_rows(2)
    weights_here(0, 1)
    mm(1, 0, 2, 1)
    send_rows(3)
    mm(0, 0, 2, 2, fresh=True)
    fetch(1)
    send_rows(4)
    with scope("know"):
        told(0)
    tell(1)
    for p in (2, 1, 0):
        weights_start(1, p)
    fetch(2)
    earlier_frame(0, 1)
    weights_here(0, 0)
    with scope("widen"):
        widen(0, 1)
    mm(1, 0, 1, 0)
    forward(0, 0)
    send_rows(5, 6)
    next_frame(1)
    send_rows(7)
    mm(0, 0, 1, 1)
    with scope("know"):
        told(1)
    tell(2)
    send_rows(8)
    fetch(3)
    rbuf[h] = sbuf[h]
    up_in.start()
    earlier_frame(0, 0)
    send_rows(9)
    with scope("widen"):
        widen(0, 0)
    mm(0, 0, 0, 0)
    next_frame(0)
    forward(1, 1)
    send_rows(10)
    with scope("know"):
        told(2)
    tell(3)
    rows_of(1, 3)
    send_rows(11)
    weights_here(1, 2)
    mm(1, 1, 3, 2, fresh=True)
    send_rows(12)
    rows_of(1, 2)
    send_rows(13)
    weights_here(1, 1)
    mm(1, 1, 2, 1)
    send_rows(14)
    mm(0, 1, 2, 2, fresh=True)
    send_rows(15)
    with scope("know"):
        told(3)
    for i in range(1, NH):
        pl.semaphore_signal(know.at[4], inc=1, device_id=(t, at_h(i)), device_id_type=MESH)
    earlier_frame(1, 1)
    weights_here(1, 0)
    with scope("widen"):
        widen(1, 1)
    mm(1, 1, 1, 0)
    forward(1, 0)
    for i in range(4):
        enc[pl.ds(512 + i * 128, 128)] = finish(1, i, first[1, i])
    mm(0, 1, 1, 1)
    for dt in range(1, NT):
        key_copy(dt).start()
    pltpu.make_async_copy(rcodes.at[t], crecv.at[:, t], kr_sem).start()
    with scope("placed"):
        for b in range(4):
            rows = pl.ds(b * 512, 512)
            placed[rows] = jnp.dot(place[rows, 512:], enc[512:], preferred_element_type=F32)
    earlier_frame(1, 0)
    with scope("widen"):
        widen(1, 0)
    mm(0, 1, 0, 0)
    for i in range(4):
        enc[pl.ds(i * 128, 128)] = finish(0, i, first[0, i])
    with scope("know"):
        pl.semaphore_wait(know.at[4], NH - 1)

    with scope("wait_rows"):
        bytes_of(rbuf.at[pl.ds(0, NH - 1)], rr_sem)

    for chip in range(4):
        to_x = lax.rem(lax.div(h, 2) + STEPS[2 * chip][0], 4)
        rows = pl.ds(pl.multiple_of(to_x * 512, 512), 512)
        with scope("terms"):
            total = placed[rows] + jnp.dot(
                place[rows, :512], enc[:512], preferred_element_type=F32
            )
            pair = rbuf[pl.ds(to_x * 2, 2)].reshape(512, C)
            tsend[rows] = (pair.astype(F32) - total).astype(BF16)

        @pl.loop(0, NT)
        def _(k):
            term_copy(2 * chip, k).start()
            if chip < 3:
                term_copy(2 * chip + 1, k).start()
            else:

                @pl.when(k < NT - 1)
                def _():
                    term_copy(NH - 1, k).start()

    pltpu.make_async_copy(
        tsend.at[pl.ds(pl.multiple_of((h * NT + t) * CAP, CAP), CAP)],
        trecv.at[pl.ds(pl.multiple_of(((NH - 1) * NT + t) * CAP, CAP), CAP)],
        gr_sem.at[3],
    ).start()

    with scope("spread"):
        make_spread()

    with scope("grad"):
        up_in.wait()
        rows_all = rbuf[...].reshape(SLOTS, C)
        for j in range(8):
            pick = pick_rows(column(slot[pl.ds(j, 1), :].astype(F32)), SLOTS // 128)
            quant = jnp.dot(pick, rows_all, preferred_element_type=F32)
            cells = pl.ds(j * 128, 128)
            grad_out[cells] = rotate_back(
                enc[cells].astype(F32), quant, up[cells].astype(F32)
            ).astype(BF16)
    grad_done = pltpu.make_async_copy(grad_out, grad_hbm, out_sem.at[0])
    grad_done.start()

    bytes_of(msg.at[pl.ds(0, OWN - NT)], cs_sem)
    bytes_of(rbuf.at[pl.ds(0, NH - 1)], rs_sem)
    bytes_of(rcodes.at[pl.ds(0, NT - 1)], ks_sem)
    for d in range(2):

        @pl.when(gives_x(d))
        def _():
            bytes_of(ext.at[0, 0, pl.ds(0, 4)], xs_sem.at[d])

        @pl.when(jnp.logical_and(t > 0, gives_x(d)))
        def _():
            bytes_of(ext.at[0, 0, pl.ds(0, 4)], xs_sem.at[2 + d])

    @pl.when(t < NT - 1)
    def _():
        bytes_of(rbuf, ts_sem)

    def arrived(chip):
        part = pl.ds(chip * 512, 512)
        with scope(f"wait_terms{chip}"):
            pltpu.make_async_copy(trecv.at[part], trecv.at[part], gr_sem.at[chip]).wait()

    def summed(rows, part):
        return jnp.dot(spread_in[rows, part], trecv[part], preferred_element_type=F32)

    arrived(0)
    with scope("sums"):
        for b in range(4):
            rows = pl.ds(b * 512, 512)
            sums[rows] = summed(rows, pl.ds(0, 512))
    sent = pl.ds(0, SLOTS - CAP)
    with scope("sent"):
        pltpu.make_async_copy(tsend.at[sent], tsend.at[sent], gs_sem).wait()
    arrived(1)
    with scope("sums"):
        for b in range(4):
            rows = pl.ds(b * 512, 512)
            sums[rows] += summed(rows, pl.ds(512, 512))
    arrived(2)
    arrived(3)
    done = []
    with scope("sums"):
        for b in range(2):
            rows = pl.ds(b * 1024, 1024)
            total = sums[rows] + summed(rows, pl.ds(1024, 1024))
            sums_out[rows] = (2.0 * total).astype(BF16)
            for n in range(2):
                rows = pl.ds(b * 1024 + n * 512, 512)
                copy = pltpu.make_async_copy(
                    sums_out.at[rows], sums_hbm.at[rows], out_sem.at[1 + 2 * b + n]
                )
                copy.start()
                done.append(copy)
    with scope("out"):
        grad_done.wait()
        for copy in done:
            copy.wait()


def window(latents, w1, w2, book, codes, upstream):
    hbm = pl.BlockSpec(memory_space=pl.ANY)
    dma = pltpu.SemaphoreType.DMA
    return pl.pallas_call(
        window_kernel,
        out_shape=(
            jax.ShapeDtypeStruct((CELLS, C), BF16),
            jax.ShapeDtypeStruct((K_OWN, C), BF16),
        ),
        in_specs=[hbm] * 6,
        out_specs=(hbm, hbm),
        scratch_shapes=[
            pltpu.VMEM((2, 4, 128, C), BF16),
            pltpu.VMEM((CELLS, C), BF16),
            pltpu.VMEM((8, 128), I32),
            pltpu.VMEM((2, 3, 3 * C, 3 * C), BF16),
            pltpu.VMEM((2, 4, 6, 128, C), BF16),
            pltpu.VMEM((4, 512, 3 * C), BF16),
            pltpu.VMEM((2, 512, 3 * C), F32),
            pltpu.VMEM((2, 4, 128, C), BF16),
            pltpu.VMEM((CELLS, C), BF16),
            pltpu.VMEM((OWN, 128), I32),
            pltpu.VMEM((8, 128), I32),
            pltpu.VMEM((NT, NH, 128), I32),
            pltpu.VMEM((8, K_OWN, C), BF16),
            pltpu.VMEM((NH, 256, C), BF16),
            pltpu.VMEM((NH, 256, C), BF16),
            pltpu.VMEM((SLOTS, CELLS), BF16),
            pltpu.VMEM((SLOTS, C), F32),
            pltpu.VMEM((SLOTS, C), BF16),
            pltpu.VMEM((SLOTS, C), BF16),
            pltpu.VMEM((NH, NT, 128), I32),
            pltpu.VMEM((K_OWN, SLOTS), BF16),
            pltpu.VMEM((K_OWN, C), F32),
            pltpu.VMEM((K_OWN, C), BF16),
            pltpu.VMEM((CELLS, C), BF16),
            dma((4,)),
            dma((2, 3)),
            dma((4,)),
            dma((2, 4, 2)),
            dma,
            dma((2, 2, 3)),
            dma,
            dma,
            dma((8,)),
            dma,
            dma,
            dma,
            dma,
            dma,
            dma((4,)),
            dma((5,)),
            pltpu.SemaphoreType.REGULAR((5,)),
        ],
        compiler_params=pltpu.CompilerParams(
            collective_id=0, has_side_effects=True, vmem_limit_bytes=VMEM_LIMIT
        ),
        name="window",
    )(latents, w1, w2, book, codes, upstream)


def hand_kernel(grad_in, sums_in, grad_ref, sums_ref, grad_buf, sums_buf, in_sem, out_sem):
    pieces = [(grad_in, grad_buf, grad_ref, k) for k in range(2)] + [
        (sums_in, sums_buf, sums_ref, k) for k in range(4)
    ]
    ins, outs = [], []
    for n, (src, buf, dst, k) in enumerate(pieces):
        rows = pl.ds(k * 512, 512)
        ins.append(pltpu.make_async_copy(src.at[rows], buf.at[rows], in_sem.at[n]))
        outs.append(pltpu.make_async_copy(buf.at[rows], dst.at[rows], out_sem.at[n]))
        ins[-1].start()
    for n in range(len(pieces)):
        ins[n].wait()
        outs[n].start()
    for n in range(len(pieces)):
        outs[n].wait()


def hand_over(grad, sums):
    hbm = pl.BlockSpec(memory_space=pl.ANY)
    dma = pltpu.SemaphoreType.DMA
    return pl.pallas_call(
        hand_kernel,
        out_shape=(
            jax.ShapeDtypeStruct((CELLS, C), BF16),
            jax.ShapeDtypeStruct((K_OWN, C), BF16),
        ),
        in_specs=[hbm, hbm],
        out_specs=(hbm, hbm),
        scratch_shapes=[
            pltpu.VMEM((CELLS, C), BF16),
            pltpu.VMEM((K_OWN, C), BF16),
            dma((6,)),
            dma((6,)),
        ],
        name="hand_over",
    )(grad, sums)


def on_device(latents, conv_first, conv_second, codebook, codes, upstream):
    grad, sums = window(
        latents,
        conv_first,
        conv_second,
        codebook,
        codes.reshape(8, 128),
        upstream.reshape(CELLS, C),
    )
    grad, sums = hand_over(grad, sums)
    return grad.reshape(upstream.shape), sums


def solution(mesh):
    return jax.shard_map(
        on_device,
        mesh=mesh,
        in_specs=(
            P("tm", "height", None, None),
            P(),
            P(),
            P("height", None),
            P("tm", "height", None),
            P("tm", "height", None, None),
        ),
        out_specs=(P("tm", "height", None, None), P(("height", "tm"), None)),
        check_vma=False,
    )
```
